256 devices in a mesh: pairs: 32 (over z, y_hi, core), aux: 8 (over x, y_lo).
Axes of the slice: x: 4, y: 4 (y_hi: 2, y_lo: 2; y = y_hi * 2 + y_lo), z: 8, core: 2. Of those that a mesh axis runs over, the one named last changes fastest.
Arguments:
- amplitudes: float32 [64, 256, 256], P('pairs'), may hold values from -6 to 6
- factors: float32 [384, 256, 256], P('aux', 'pairs'), may hold values from -0.078125 to 0.078125
- occ_factors: float32 [384, 8, 8], P('aux'), may hold values from -0.5 to 0.5
Outputs:
- resid: float32 [64, 256, 256], P(None, 'pairs', 'aux')
The draws below stay inside these ranges and needn't reach their ends.
All inputs are finite; a program needn't handle non-finite values.
Results may differ from the reference program's by a relative error of at most 0.0001.
Values sent between devices are 32-bit elements; how exact they have to be, the bound alone decides.
A program may use at most 64 MiB of HBM per device.

```python
import jax
import jax.numpy as jnp
from jax import lax

V = 256
NAUX = 384
OW = 8
PAIRS = 64


def levels(stream_key, shape, shards, least, high):
    factor_of = 1.0
    for position, shards_of in shards:
        heights = jax.random.uniform(jax.random.fold_in(jax.random.fold_in(stream_key, 6), position), (shards_of,), jnp.float32, least / len(shards), high / len(shards))
        factor_of = factor_of * jnp.repeat(jnp.exp(heights), shape[position] // shards_of).reshape((-1,) + (1,) * (len(shape) - 1 - position))
    return factor_of


def gaussian(key, shape, deviation, limit, shards=(), dtype=jnp.bfloat16):
    factor_of = levels(key, shape, shards, -0.22, 0.18) if shards else 1.0
    values = jax.random.normal(key, shape, jnp.float32) * deviation * factor_of
    return jnp.minimum(jnp.maximum(values, -limit), limit).astype(dtype)


def setup_inputs(seed: int = 0) -> dict:
    streams_of = jax.random.split(jax.random.key(seed), 4)
    amplitudes = gaussian(streams_of[0], (PAIRS, V, V), 1.0, 6.0, ((0, 32),), jnp.float32)
    factors = gaussian(streams_of[1], (NAUX, V, V), (V * 20) ** -0.5, 0.078125, ((0, 8), (1, 32)), jnp.float32)
    occ_factors = gaussian(streams_of[2], (NAUX, OW, OW), (OW * 20) ** -0.5, 0.5, ((0, 8),), jnp.float32)
    return dict(amplitudes=amplitudes, factors=factors, occ_factors=occ_factors)


highest = lax.Precision.HIGHEST


def reference(amplitudes, factors, occ_factors):
    def add_factor(running, factor):
        mixed_terms = jnp.einsum('icd,bd->icb', amplitudes, factor, precision=highest)
        return running + jnp.einsum('ac,icb->iab', factor, mixed_terms, precision=highest), None

    particle, unused = lax.scan(add_factor, jnp.zeros(amplitudes.shape, jnp.float32), factors)
    coupling = jnp.einsum('pik,pjl->ijkl', occ_factors, occ_factors, precision=highest).reshape(PAIRS, PAIRS)
    ladder = particle + jnp.einsum('pk,kab->pab', coupling, amplitudes, precision=highest)
    flipped = jnp.swapaxes(ladder, 1, 2).reshape(OW, OW, V, V).transpose(1, 0, 2, 3).reshape(PAIRS, V, V)
    return ladder + flipped
```

```python
import functools

import jax
import jax.numpy as jnp
from jax import lax
from jax.experimental import pallas as pl
from jax.experimental.pallas import tpu as pltpu
from jax.sharding import PartitionSpec as P

highest = lax.Precision.HIGHEST
F32 = jnp.float32
BF16 = jnp.bfloat16

Z = 8
K = 4
W = 8
PLANE = K * W
OFFSETS = 5
CHUNKS = 4


def remote(src, dst, send_sem, recv_sem, p, w):
    return pltpu.make_async_remote_copy(
        src_ref=src,
        dst_ref=dst,
        send_sem=send_sem,
        recv_sem=recv_sem,
        device_id={"pairs": p, "aux": w},
        device_id_type=pl.DeviceIdType.MESH,
    )


def wait_bytes(ref, sem):
    pltpu.make_async_copy(ref, ref, sem).wait()


def place():
    p = lax.axis_index("pairs")
    w = lax.axis_index("aux")
    return p, w, p // K, lax.rem(p, K)


def greet(p, w, z):
    barrier = pltpu.get_barrier_semaphore()
    k = lax.rem(p, K)
    m = w * K + k

    def plane_peer(t, c):
        n = lax.rem(m + t, PLANE)
        pl.semaphore_signal(
            barrier, inc=1, device_id={"pairs": z * K + lax.rem(n, K), "aux": n // K},
            device_id_type=pl.DeviceIdType.MESH)
        return c

    def column_peer(t, c):
        pl.semaphore_signal(
            barrier, inc=1, device_id={"pairs": lax.rem(p + t, Z * K), "aux": w},
            device_id_type=pl.DeviceIdType.MESH)
        return c

    lax.fori_loop(1, PLANE, plane_peer, 0)
    lax.fori_loop(1, Z * K, column_peer, 0)
    pl.semaphore_wait(barrier, PLANE + Z * K - 2)


def gather_kernel(amp, fac, ball, sall, flip, slots, mine,
                  ex_send, ex_recv, a_send, a_recv, s_send, s_recv, ring_send, ring_recv):
    p, w, z, k = place()
    m = w * K + k
    greet(p, w, z)
    per = ball.shape[0] // CHUNKS
    up = lax.rem(z + 1, Z) * K + k
    down = lax.rem(z + Z - 1, Z) * K + k

    def exchange(g, t):
        kk = lax.rem(k + t, K)
        src = fac.at[pl.ds(kk * (per * CHUNKS) + g * per, per)]
        dst = ball.at[pl.ds(g * per, per), pl.ds(pl.multiple_of(8 * p, 8), 8), :]
        if t == 0:
            return pltpu.make_async_copy(src, dst, ex_recv.at[g])
        return remote(src, dst, ex_send.at[g], ex_recv.at[g], z * K + kk, w)

    for g in range(CHUNKS):
        for t in range(K):
            exchange(g, t).start()

    def straight(t):
        kk = lax.rem(k + t, K)
        src = amp.at[:, pl.ds(pl.multiple_of((w * K + kk) * 8, 8), 8), :]
        dst = slots.at[pl.ds(2 * k, 2)]
        if t == 0:
            return pltpu.make_async_copy(src, dst, a_recv)
        return remote(src, dst, a_send, a_recv, z * K + kk, w)

    def turned(s, kk):
        src = flip.at[s, pl.ds(pl.multiple_of((w * K + kk) * 8, 8), 8), :]
        dst = slots.at[Z + z]
        near = pltpu.make_async_copy(src, dst, a_recv)
        far = remote(src, dst, a_send, a_recv, (2 * k + s) * K + kk, w)
        return near, far, jnp.logical_and(2 * k + s == z, kk == k)

    for t in range(K):
        straight(t).start()
    for s in range(2):
        flip[s] = amp[s].T
    for s in range(2):
        for kk in range(K):
            near, far, here = turned(s, kk)
            pl.when(here)(near.start)
            pl.when(jnp.logical_not(here))(far.start)

    def hops(way, g):
        return 4 if (way + g) % 2 == 0 else 3

    def ring(way, g, h):
        origin = lax.rem(z + (Z - h if way == 0 else h), Z)
        part = ball.at[pl.ds(g * per, per), pl.ds(pl.multiple_of(origin * 32, 32), 32), :]
        return remote(part, part, ring_send.at[way, g, h], ring_recv.at[way, g, h], up if way == 0 else down, w)

    def arrived(way, g, h):
        origin = lax.rem(z + (Z - 1 - h if way == 0 else 1 + h), Z)
        part = ball.at[pl.ds(g * per, per), pl.ds(pl.multiple_of(origin * 32, 32), 32), :]
        return remote(part, part, ring_send.at[way, g, h], ring_recv.at[way, g, h], up if way == 0 else down, w)

    for g in range(CHUNKS):
        wait_bytes(ball.at[pl.ds(g * per, per), pl.ds(pl.multiple_of(z * 32, 32), 32), :], ex_recv.at[g])
        for way in range(2):
            ring(way, g, 0).start()

    wait_bytes(slots, a_recv)
    for d in range(OFFSETS):
        j = lax.rem(z + d, Z)
        mine[d] = slots[j] + slots[Z + j]

    def share(t):
        n = lax.rem(m + t, PLANE)
        return remote(mine, sall.at[:, pl.ds(pl.multiple_of(m * 8, 8), 8), :], s_send, s_recv,
                      z * K + lax.rem(n, K), n // K)

    pltpu.make_async_copy(mine, sall.at[:, pl.ds(pl.multiple_of(m * 8, 8), 8), :], s_recv).start()

    def share_start(t, c):
        share(t).start()
        return c

    lax.fori_loop(1, PLANE, share_start, 0)

    for h in range(1, 4):
        for g in range(CHUNKS):
            for way in range(2):
                if h < hops(way, g):
                    arrived(way, g, h - 1).wait_recv()
                    ring(way, g, h).start()
    for g in range(CHUNKS):
        for way in range(2):
            arrived(way, g, hops(way, g) - 1).wait_recv()
    wait_bytes(sall, s_recv)
    for g in range(CHUNKS):
        for t in range(1, K):
            exchange(g, t).wait_send()
        for way in range(2):
            for h in range(hops(way, g)):
                ring(way, g, h).wait_send()
    for t in range(1, K):
        straight(t).wait_send()
    for s in range(2):
        for kk in range(K):
            near, far, here = turned(s, kk)
            pl.when(jnp.logical_not(here))(far.wait_send)
    wait_bytes(sall.at[:, pl.ds(0, 8 * (PLANE - 1)), :], s_send)


def gather(amplitudes, factors):
    aux_local, rows, virt = factors.shape
    local = aux_local // K
    vm = pl.BlockSpec(memory_space=pltpu.VMEM)
    dma = pltpu.SemaphoreType.DMA
    return pl.pallas_call(
        gather_kernel,
        out_shape=(
            jax.ShapeDtypeStruct((local, virt, virt), F32),
            jax.ShapeDtypeStruct((OFFSETS, virt, virt), F32),
        ),
        in_specs=[vm, vm],
        out_specs=(vm, vm),
        scratch_shapes=[
            pltpu.VMEM((2, virt, virt), F32),
            pltpu.VMEM((2 * Z, 8, virt), F32),
            pltpu.VMEM((OFFSETS, 8, virt), F32),
            dma((CHUNKS,)), dma((CHUNKS,)),
            dma(()), dma(()), dma(()), dma(()),
            dma((2, CHUNKS, 4)), dma((2, CHUNKS, 4)),
        ],
        compiler_params=pltpu.CompilerParams(
            collective_id=0, has_side_effects=True, vmem_limit_bytes=40 << 20),
        name="gather",
    )(amplitudes, factors)


def split(x):
    hi = x.astype(BF16)
    return hi, (x - hi.astype(F32)).astype(BF16)


def dot(a, b):
    return lax.dot_general(a, b, (((1,), (0,)), ((), ())), preferred_element_type=F32)


def dot_t(a, b):
    return lax.dot_general(a, b, (((1,), (1,)), ((), ())), preferred_element_type=F32)


def ladder_kernel(ball, sall, out, s_hi, s_lo, y_hi, y_lo, acc):
    per = y_hi.shape[0]
    virt = ball.shape[1]
    for d in range(OFFSETS):
        s_hi[d], s_lo[d] = split(sall[d])

    def chunk(g, c):
        b_hi, b_lo = split(ball[pl.ds(g * per, per)].reshape(per * virt, virt))
        for d in range(OFFSETS):
            y = dot(b_hi, s_hi[d]) + dot(b_hi, s_lo[d]) + dot(b_lo, s_hi[d])
            hi, lo = split(y)
            for q in range(per):
                y_hi[q, d * virt:(d + 1) * virt] = hi[q * virt:(q + 1) * virt]
                y_lo[q, d * virt:(d + 1) * virt] = lo[q * virt:(q + 1) * virt]
        total = None
        for q in range(per):
            bh, bl = b_hi[q * virt:(q + 1) * virt], b_lo[q * virt:(q + 1) * virt]
            term = dot_t(y_hi[q], bh) + dot_t(y_hi[q], bl) + dot_t(y_lo[q], bh)
            total = term if total is None else total + term
        acc[...] += total
        return c

    acc[...] = jnp.zeros_like(acc)
    lax.fori_loop(0, ball.shape[0] // per, chunk, 0)
    for d in range(OFFSETS):
        r = acc[d * virt:(d + 1) * virt]
        if d < 4:
            out[d] = r
        else:
            out[7] = r
        if 1 <= d <= 3:
            out[3 + d] = r.T


def ladder(ball, sall):
    virt = ball.shape[1]
    per = 3
    vm = pl.BlockSpec(memory_space=pltpu.VMEM)
    return pl.pallas_call(
        ladder_kernel,
        out_shape=jax.ShapeDtypeStruct((Z, virt, virt), F32),
        in_specs=[vm, vm],
        out_specs=vm,
        scratch_shapes=[
            pltpu.VMEM((OFFSETS, virt, virt), BF16),
            pltpu.VMEM((OFFSETS, virt, virt), BF16),
            pltpu.VMEM((per, OFFSETS * virt, virt), BF16),
            pltpu.VMEM((per, OFFSETS * virt, virt), BF16),
            pltpu.VMEM((OFFSETS * virt, virt), F32),
        ],
        compiler_params=pltpu.CompilerParams(vmem_limit_bytes=48 << 20),
        name="ladder",
    )(ball, sall)


def where_to():
    order = []
    for z in range(Z):
        for m in range(8):
            if m < 4:
                i, j = (z + m) % 8, z
            elif m < 7:
                i, j = z, (z + m - 3) % 8
            else:
                i, j = (z + 4) % 8, z
            order.append(i * 8 + j)
    return order


def scatter_kernel(part, hole, out, sib, half, slots, turn, last,
                   c_send, c_recv, r_send, r_recv, f_send, f_recv):
    p, w, z, k = place()
    greet(p, w, z)
    core = lax.rem(k, 2)
    up_half = k // 2
    other = p + 1 - 2 * core
    virt = part.shape[1]
    rows = virt // W

    def swap(v):
        return remote(part.at[pl.ds(4 * v + 2 * (1 - core), 2)], sib.at[pl.ds(2 * v, 2)],
                      c_send.at[v], c_recv.at[v], other, w)

    for v in range(2):
        swap(v).start()
    for v in range(2):
        swap(v).wait_recv()
        half[2 * v:2 * v + 2] = part[pl.ds(4 * v + 2 * core, 2)] + sib[2 * v:2 * v + 2]

    me = up_half * W + w

    def spread(t):
        n = lax.rem(me + t, 2 * W)
        v, ww = n // W, lax.rem(n, W)
        src = half.at[pl.ds(2 * v, 2), pl.ds(pl.multiple_of(ww * rows, rows), rows), :]
        return src, v, ww

    def spread_start(t, c):
        src, v, ww = spread(t)
        remote(src, slots.at[me], r_send, r_recv, z * K + v * 2 + core, ww).start()
        return c

    own, _, _ = spread(0)
    pltpu.make_async_copy(own, slots.at[me], r_recv).start()
    lax.fori_loop(1, 2 * W, spread_start, 0)
    wait_bytes(slots, r_recv)
    for s in range(2):
        total = slots[0, s]
        for n in range(1, 2 * W):
            total = total + slots[n, s]
        turn[s] = total.T

    def final(t):
        q = lax.rem(p + t, Z * K)
        return turn.at[:, pl.ds(pl.multiple_of(q * 8, 8), 8), :], q

    def final_start(t, c):
        src, q = final(t)
        remote(src, last.at[pl.ds(2 * p, 2)], f_send, f_recv, q, w).start()
        return c

    mine, _ = final(0)
    pltpu.make_async_copy(mine, last.at[pl.ds(2 * p, 2)], f_recv).start()
    lax.fori_loop(1, Z * K, final_start, 0)
    wait_bytes(last, f_recv)
    for slot, pair in enumerate(where_to()):
        out[pair] = last[slot] + hole[pair]
    for v in range(2):
        swap(v).wait_send()
    wait_bytes(slots.at[pl.ds(0, 2 * W - 1)], r_send)
    wait_bytes(last.at[pl.ds(0, 2 * (Z * K - 1))], f_send)


def scatter(part, hole):
    virt = part.shape[1]
    rows = virt // W
    vm = pl.BlockSpec(memory_space=pltpu.VMEM)
    dma = pltpu.SemaphoreType.DMA
    return pl.pallas_call(
        scatter_kernel,
        out_shape=jax.ShapeDtypeStruct(hole.shape, F32),
        in_specs=[vm, vm],
        out_specs=vm,
        scratch_shapes=[
            pltpu.VMEM((4, virt, virt), F32),
            pltpu.VMEM((4, virt, virt), F32),
            pltpu.VMEM((2 * W, 2, rows, virt), F32),
            pltpu.VMEM((2, virt, rows), F32),
            pltpu.VMEM((2 * Z * K, 8, rows), F32),
            dma((2,)), dma((2,)), dma(()), dma(()), dma(()), dma(()),
        ],
        compiler_params=pltpu.CompilerParams(
            collective_id=1, has_side_effects=True, vmem_limit_bytes=40 << 20),
        name="scatter",
    )(part, hole)


def hole_ladder(amplitudes, occ_factors):
    virt = amplitudes.shape[1]
    occupied = occ_factors.shape[1]
    pairs = occupied * occupied
    columns = virt // lax.axis_size("aux")
    start = lax.axis_index("aux") * columns
    cols = lax.dynamic_slice_in_dim(amplitudes, start, columns, 2)
    flip = jnp.swapaxes(lax.dynamic_slice_in_dim(amplitudes, start, columns, 1), 1, 2)
    cols = lax.all_to_all(cols, "pairs", split_axis=1, concat_axis=0, tiled=True)
    flip = lax.all_to_all(flip, "pairs", split_axis=1, concat_axis=0, tiled=True)
    rows = cols.shape[1]
    flip = flip.reshape(occupied, occupied, rows, columns).transpose(1, 0, 2, 3).reshape(pairs, rows, columns)
    coupling = jnp.einsum("pik,pjl->ijkl", occ_factors, occ_factors, precision=highest).reshape(pairs, pairs)
    coupling = lax.psum(coupling, "aux")
    return jnp.einsum("pk,kab->pab", coupling, cols + flip, precision=highest)


def shards(amplitudes, factors, occ_factors):
    hole = hole_ladder(amplitudes, occ_factors)
    ball, sall = gather(amplitudes, factors)
    part = ladder(ball, sall)
    return scatter(part, hole)


def solution(mesh):
    placed = (P("pairs", None, None), P("aux", "pairs", None), P("aux", None, None))
    return jax.shard_map(
        shards, mesh=mesh, in_specs=placed, out_specs=P(None, "pairs", "aux"), check_vma=False
    )
```

```python
import jax
import jax.numpy as jnp
from jax import lax
from jax.experimental import pallas as pl
from jax.experimental.pallas import tpu as pltpu
from jax.sharding import PartitionSpec as P

highest = lax.Precision.HIGHEST
F32 = jnp.float32
BF16 = jnp.bfloat16

Z = 8
K = 4
W = 8
PLANE = K * W
CHIPS = PLANE // 2
OFFSETS = 5
CHUNKS = 6


def remote(src, dst, send_sem, recv_sem, p, w):
    return pltpu.make_async_remote_copy(
        src_ref=src,
        dst_ref=dst,
        send_sem=send_sem,
        recv_sem=recv_sem,
        device_id={"pairs": p, "aux": w},
        device_id_type=pl.DeviceIdType.MESH,
    )


def wait_bytes(ref, sem):
    pltpu.make_async_copy(ref, ref, sem).wait()


def greet(p, w, z, k):
    barrier = pltpu.get_barrier_semaphore()
    m = w * K + k

    def plane_peer(t, c):
        n = lax.rem(m + t, PLANE)
        pl.semaphore_signal(
            barrier, inc=1, device_id={"pairs": z * K + lax.rem(n, K), "aux": n // K},
            device_id_type=pl.DeviceIdType.MESH)
        return c

    def column_peer(t, c):
        pl.semaphore_signal(
            barrier, inc=1, device_id={"pairs": lax.rem(p + t, Z * K), "aux": w},
            device_id_type=pl.DeviceIdType.MESH)
        return c

    lax.fori_loop(1, PLANE, plane_peer, 0)
    lax.fori_loop(1, Z * K, column_peer, 0)
    pl.semaphore_wait(barrier, PLANE + Z * K - 2)


def split(x):
    hi = x.astype(BF16)
    return hi, (x - hi.astype(F32)).astype(BF16)


def dot(a, b):
    return lax.dot_general(a, b, (((1,), (0,)), ((), ())), preferred_element_type=F32)


def dot_t(a, b, precision=None):
    return lax.dot_general(a, b, (((1,), (1,)), ((), ())), preferred_element_type=F32, precision=precision)


def loop(start, stop, body):
    def step(t, c):
        body(t)
        return c

    lax.fori_loop(start, stop, step, 0)


def kernel(amp_hbm, fac, occ, out,
           amp, flip, slots, mine, sall, ball, s_hi, s_lo, b_hi, b_lo, y_hi, y_lo, acc,
           sib, half, parts, tall, at, gb, slot_a, slot_b, hd, hr, occs, gm, cm, hs, hout,
           in_sem, ex_send, ex_recv, a_send, a_recv, s_send, s_recv, w_send, w_recv, ring_send, ring_recv,
           q_send, q_recv, h_send, h_recv, c_send, c_recv, r_send, r_recv, f_send, f_recv, g_send, g_recv):
    p = lax.axis_index("pairs")
    w = lax.axis_index("aux")
    z, k = p // K, lax.rem(p, K)
    core = lax.rem(k, 2)
    m = w * K + k
    chip = w * 2 + k // 2
    other = p + 1 - 2 * core
    virt = amp.shape[1]
    cols = virt // W
    per = ball.shape[0] // CHUNKS
    up = lax.rem(z + 1, Z) * K + k
    down = lax.rem(z + Z - 1, Z) * K + k

    load = pltpu.make_async_copy(amp_hbm, amp, in_sem)
    load.start()
    greet(p, w, z, k)

    def exchange(g, t):
        kk = lax.rem(k + t, K)
        src = fac.at[pl.ds(kk * (per * CHUNKS) + g * per, per)]
        dst = ball.at[pl.ds(g * per, per), pl.ds(pl.multiple_of(8 * p, 8), 8), :]
        if t == 0:
            return pltpu.make_async_copy(src, dst, ex_recv.at[g])
        return remote(src, dst, ex_send.at[g], ex_recv.at[g], z * K + kk, w)

    for g in range(CHUNKS):
        for t in range(K):
            exchange(g, t).start()

    def straight(t):
        kk = lax.rem(k + t, K)
        src = amp.at[:, pl.ds(pl.multiple_of((w * K + kk) * 8, 8), 8), :]
        dst = slots.at[pl.ds(2 * k, 2)]
        if t == 0:
            return pltpu.make_async_copy(src, dst, a_recv)
        return remote(src, dst, a_send, a_recv, z * K + kk, w)

    def turned_far(s, kk):
        src = flip.at[s, pl.ds(pl.multiple_of((w * K + kk) * 8, 8), 8), :]
        return remote(src, slots.at[Z + z], a_send, a_recv, (2 * k + s) * K + kk, w)

    def turned_near(s, kk):
        src = flip.at[s, pl.ds(pl.multiple_of((w * K + kk) * 8, 8), 8), :]
        return pltpu.make_async_copy(src, slots.at[Z + z], a_recv)

    load.wait()
    for t in range(K):
        straight(t).start()
    for s in range(2):
        flip[s] = amp[s].T
    for s in range(2):
        for kk in range(K):
            here = jnp.logical_and(2 * k + s == z, kk == k)
            pl.when(here)(lambda s=s, kk=kk: turned_near(s, kk).start())
            pl.when(jnp.logical_not(here))(lambda s=s, kk=kk: turned_far(s, kk).start())

    def hops(way, g):
        return 4 if (way + g) % 2 == 0 else 3

    def ring(way, g, h):
        origin = lax.rem(z + (Z - h if way == 0 else h), Z)
        part = ball.at[pl.ds(g * per, per), pl.ds(pl.multiple_of(origin * 32, 32), 32), :]
        return remote(part, part, ring_send.at[way, g, h], ring_recv.at[way, g, h], up if way == 0 else down, w)

    def arrive(way, g, h):
        origin = lax.rem(z + (Z - 1 - h if way == 0 else 1 + h), Z)
        part = ball.at[pl.ds(g * per, per), pl.ds(pl.multiple_of(origin * 32, 32), 32), :]
        remote(part, part, ring_send.at[way, g, h], ring_recv.at[way, g, h],
               up if way == 0 else down, w).wait_recv()

    def own(g):
        wait_bytes(ball.at[pl.ds(g * per, per), pl.ds(pl.multiple_of(z * 32, 32), 32), :], ex_recv.at[g])
        for way in range(2):
            ring(way, g, 0).start()

    def forward(g, parity, h):
        for way in range(2):
            if h < hops(way, parity):
                arrive(way, g, h - 1)
                ring(way, g, h).start()

    own(0)
    own(1)

    wait_bytes(slots, a_recv)
    for d in range(OFFSETS):
        j = lax.rem(z + d, Z)
        mine[d] = slots[j] + slots[Z + j]

    def share(t):
        n = lax.rem(chip + t, CHIPS)
        return remote(mine, sall.at[:, chip, core], s_send, s_recv, z * K + lax.rem(n, 2) * 2 + core, n // 2)

    pltpu.make_async_copy(mine, sall.at[:, chip, core], s_recv).start()
    loop(1, CHIPS, lambda t: share(t).start())
    forward(0, 0, 1)

    def occ_share(t):
        return remote(occ, occs.at[w], q_send, q_recv, p, lax.rem(w + t, W))

    pltpu.make_async_copy(occ, occs.at[w], q_recv).start()
    loop(1, W, lambda t: occ_share(t).start())

    at_w = pl.ds(pl.multiple_of(w * cols, cols), cols)
    for s in range(2):
        hd[:, s * cols:(s + 1) * cols] = flip[s, at_w, :].T
        hd[:, (2 + s) * cols:(3 + s) * cols] = amp[s, at_w, :].T
    forward(1, 1, 1)
    forward(0, 0, 2)
    forward(0, 0, 3)

    wait_bytes(sall.at[:, :, core], s_recv)
    across = remote(sall.at[:, :, core], sall.at[:, :, core], w_send, w_recv, other, w)
    across.start()
    acc[...] = jnp.zeros_like(acc)
    wait_bytes(sall.at[:, :, 1 - core], w_recv)
    for d in range(OFFSETS):
        s_hi[d], s_lo[d] = split(sall[d].reshape(virt, virt))

    def first(d):
        bh, bl = b_hi[...], b_lo[...]
        hi, lo = split(dot(bh, s_hi[d]) + dot(bh, s_lo[d]) + dot(bl, s_hi[d]))
        for q in range(per):
            y_hi[q, d * virt:(d + 1) * virt] = hi[q * virt:(q + 1) * virt]
            y_lo[q, d * virt:(d + 1) * virt] = lo[q * virt:(q + 1) * virt]

    def second(q):
        bh, bl = b_hi[q * virt:(q + 1) * virt], b_lo[q * virt:(q + 1) * virt]
        acc[...] += dot_t(y_hi[q], bh) + dot_t(y_hi[q], bl) + dot_t(y_lo[q], bh)

    def chunk_pair(g2):
        for u in range(2):
            g = 2 * g2 + u
            for way in range(2):
                arrive(way, g, hops(way, u) - 1)
            b_hi[...], b_lo[...] = split(ball[pl.ds(g * per, per)].reshape(per * virt, virt))
            pl.when(g + 2 < CHUNKS)(lambda: own(g + 2))
            first(0)
            first(1)
            pl.when(g + 1 < CHUNKS)(lambda: forward(g + 1, 1 - u, 2))
            first(2)
            first(3)
            pl.when(g + 2 < CHUNKS)(lambda: forward(g + 2, u, 1))
            first(4)
            second(0)
            pl.when(g + 1 < CHUNKS)(lambda: forward(g + 1, 1 - u, 3))
            second(1)

    loop(0, CHUNKS // 2, chunk_pair)

    sums = acc.reshape(OFFSETS, CHIPS, 2, 8, virt)
    swap = remote(sums.at[:, :, 1 - core], sib, c_send, c_recv, other, w)
    swap.start()

    def hole_send(t):
        q = lax.rem(p + t, Z * K)
        return remote(hd.at[pl.ds(pl.multiple_of(q * 8, 8), 8), :], hr.at[p], h_send, h_recv, q, w)

    pltpu.make_async_copy(hd.at[pl.ds(pl.multiple_of(p * 8, 8), 8), :], hr.at[p], h_recv).start()
    swap.wait_recv()
    half[...] = sums[:, :, core] + sib[...]

    def spread(t):
        n = lax.rem(chip + t, CHIPS)
        return remote(half.at[:, n], parts.at[chip], r_send, r_recv, z * K + lax.rem(n, 2) * 2 + core, n // 2)

    pltpu.make_async_copy(half.at[:, chip], parts.at[chip], r_recv).start()
    loop(1, CHIPS, lambda t: spread(t).start())
    loop(1, Z * K, lambda t: hole_send(t).start())

    wait_bytes(occs, q_recv)
    g_sum = dot_t(occs[0], occs[0], highest)
    for n in range(1, W):
        g_sum = g_sum + dot_t(occs[n], occs[n], highest)
    gm[...] = g_sum
    by_k = [gm[pl.ds(kk, 8, stride=8), :] for kk in range(8)]
    for j in range(8):
        cm[pl.ds(j, 8, stride=8), :] = jnp.concatenate([x[:, j * 8:j * 8 + 8] for x in by_k], axis=1)
    wait_bytes(hr, h_recv)
    flat = hr.reshape(Z * K * 8, 4 * cols)
    by_a = [flat[pl.ds(a, Z * K, stride=8), :] for a in range(8)]
    for s in range(2):
        for e in range(2):
            hs[e, pl.ds(s, Z * K, stride=2), :] = jnp.concatenate(
                [x[:, s * cols:(s + 1) * cols] for x in by_a[4 * e:4 * e + 4]], axis=1)
    for l2 in range(4):
        by_a = [flat[pl.ds(8 * l2 + a, 8, stride=32), :] for a in range(8)]
        for s in range(2):
            for e in range(2):
                at_row = 16 * l2 + 8 * s
                hs[e, at_row:at_row + 8, :] += jnp.concatenate(
                    [x[:, (2 + s) * cols:(3 + s) * cols] for x in by_a[4 * e:4 * e + 4]], axis=1)
    hole = [lax.dot_general(cm[...], hs[e], (((1,), (0,)), ((), ())), preferred_element_type=F32, precision=highest)
            for e in range(2)]
    for a in range(8):
        hout[pl.ds(a, 64, stride=8), :] = hole[a // 4][:, a % 4 * cols:(a % 4 + 1) * cols]

    wait_bytes(parts, r_recv)
    total = parts[0]
    for n in range(1, CHIPS):
        total = total + parts[n]
    tall[...] = jnp.zeros_like(tall)
    for d in range(4):
        tall[pl.ds(pl.multiple_of(d * 32 + 8 * k, 8), 8), :] = total[d]
    at[...] = tall[...].T
    for ww in range(W):
        for d in range(1, OFFSETS):
            gb[ww, :, (d - 1) * cols:d * cols] = total[d][:, ww * cols:(ww + 1) * cols]

    def col_send(t):
        q = lax.rem(p + t, Z * K)
        return remote(at.at[pl.ds(pl.multiple_of(q * 8, 8), 8), :], slot_a.at[p], f_send, f_recv, q, w)

    def row_send(ww):
        return remote(gb.at[ww], slot_b.at[z], g_send, g_recv, m, ww)

    def row_here(ww):
        return jnp.logical_and(m == p, ww == w)

    for ww in range(W):
        pl.when(row_here(ww))(lambda ww=ww: pltpu.make_async_copy(gb.at[ww], slot_b.at[z], g_recv).start())
        pl.when(jnp.logical_not(row_here(ww)))(lambda ww=ww: row_send(ww).start())
    pltpu.make_async_copy(at.at[pl.ds(pl.multiple_of(p * 8, 8), 8), :], slot_a.at[p], f_recv).start()
    loop(1, Z * K, lambda t: col_send(t).start())

    wait_bytes(slot_b, g_recv)
    for zz in range(Z):
        tile = slot_b[zz]
        for d in range(1, OFFSETS):
            pair = zz * 8 + (zz + d) % 8
            out[pair] = tile[:, (d - 1) * cols:d * cols] + hout[pair * 8:pair * 8 + 8, :]
    wait_bytes(slot_a, f_recv)
    for zz in range(Z):
        tile = slot_a[zz * K] + slot_a[zz * K + 1] + slot_a[zz * K + 2] + slot_a[zz * K + 3]
        for d in range(4):
            pair = (zz + d) % 8 * 8 + zz
            out[pair] = tile[:, d * cols:(d + 1) * cols] + hout[pair * 8:pair * 8 + 8, :]

    for g in range(CHUNKS):
        for t in range(1, K):
            exchange(g, t).wait_send()
        for way in range(2):
            for h in range(hops(way, g)):
                ring(way, g, h).wait_send()
    for t in range(1, K):
        straight(t).wait_send()
    for s in range(2):
        for kk in range(K):
            here = jnp.logical_and(2 * k + s == z, kk == k)
            pl.when(jnp.logical_not(here))(lambda s=s, kk=kk: turned_far(s, kk).wait_send())
    across.wait_send()
    swap.wait_send()
    for ww in range(W):
        pl.when(jnp.logical_not(row_here(ww)))(lambda ww=ww: row_send(ww).wait_send())
    wait_bytes(parts.at[pl.ds(0, CHIPS - 1)], s_send)
    wait_bytes(parts.at[pl.ds(0, CHIPS - 1)], r_send)
    wait_bytes(occs.at[pl.ds(0, W - 1)], q_send)
    wait_bytes(hr.at[pl.ds(0, Z * K - 1)], h_send)
    wait_bytes(slot_a.at[pl.ds(0, Z * K - 1)], f_send)


def shards(amplitudes, factors, occ_factors):
    aux_local, rows, virt = factors.shape
    occupied = occ_factors.shape[1]
    local = aux_local // K
    per = local // CHUNKS
    cols = virt // W
    occ = occ_factors.transpose(1, 2, 0).reshape(occupied * occupied, aux_local)
    vm = pl.BlockSpec(memory_space=pltpu.VMEM)
    anywhere = pl.BlockSpec(memory_space=pltpu.HBM)
    dma = pltpu.SemaphoreType.DMA
    v = pltpu.VMEM
    scratch = [
        v((2, virt, virt), F32), v((2, virt, virt), F32),
        v((2 * Z, 8, virt), F32), v((OFFSETS, 8, virt), F32),
        v((OFFSETS, CHIPS, 2, 8, virt), F32), v((local, virt, virt), F32),
        v((OFFSETS, virt, virt), BF16), v((OFFSETS, virt, virt), BF16),
        v((per * virt, virt), BF16), v((per * virt, virt), BF16),
        v((per, OFFSETS * virt, virt), BF16), v((per, OFFSETS * virt, virt), BF16),
        v((OFFSETS * virt, virt), F32),
        v((OFFSETS, CHIPS, 8, virt), F32), v((OFFSETS, CHIPS, 8, virt), F32),
        v((CHIPS, OFFSETS, 8, virt), F32),
        v((128, virt), F32), v((virt, 128), F32),
        v((W, 8, 128), F32), v((Z * K, 8, 128), F32), v((Z, 8, 128), F32),
        v((virt, 128), F32), v((Z * K, 8, 128), F32),
        v((W, occupied * occupied, aux_local), F32),
        v((64, 64), F32), v((64, 64), F32), v((2, 64, 128), F32), v((64 * 8, cols), F32),
        dma(()), dma((CHUNKS,)), dma((CHUNKS,)),
        dma(()), dma(()), dma(()), dma(()), dma(()), dma(()),
        dma((2, CHUNKS, 4)), dma((2, CHUNKS, 4)),
        dma(()), dma(()), dma(()), dma(()), dma(()), dma(()), dma(()), dma(()), dma(()), dma(()), dma(()), dma(()),
    ]
    return pl.pallas_call(
        kernel,
        out_shape=jax.ShapeDtypeStruct((occupied * occupied, rows, cols), F32),
        in_specs=[anywhere, anywhere, vm],
        out_specs=vm,
        scratch_shapes=scratch,
        compiler_params=pltpu.CompilerParams(
            collective_id=0, has_side_effects=True, vmem_limit_bytes=52 << 20),
        name="residual",
    )(amplitudes, factors, occ)


def solution(mesh):
    placed = (P("pairs", None, None), P("aux", "pairs", None), P("aux", None, None))
    return jax.shard_map(
        shards, mesh=mesh, in_specs=placed, out_specs=P(None, "pairs", "aux"), check_vma=False
    )
```

```python
import jax
import jax.numpy as jnp
from jax import lax
from jax.experimental import pallas as pl
from jax.experimental.pallas import tpu as pltpu
from jax.sharding import PartitionSpec as P

highest = lax.Precision.HIGHEST
F32 = jnp.float32
BF16 = jnp.bfloat16

Z = 8
K = 4
W = 8
PLANE = K * W
CHIPS = PLANE // 2
OFFSETS = 5
GROUPS = ((0, 6), (6, 6))


def remote(src, dst, send_sem, recv_sem, p, w):
    return pltpu.make_async_remote_copy(
        src_ref=src,
        dst_ref=dst,
        send_sem=send_sem,
        recv_sem=recv_sem,
        device_id={"pairs": p, "aux": w},
        device_id_type=pl.DeviceIdType.MESH,
    )


def wait_bytes(ref, sem):
    pltpu.make_async_copy(ref, ref, sem).wait()


def greet(p, w, z, core, chip):
    barrier = pltpu.get_barrier_semaphore()

    def plane_peer(t):
        n = lax.rem(chip + t, CHIPS)
        pl.semaphore_signal(
            barrier, inc=1, device_id={"pairs": z * K + lax.rem(n, 2) * 2 + core, "aux": n // 2},
            device_id_type=pl.DeviceIdType.MESH)

    def column_peer(t):
        pl.semaphore_signal(
            barrier, inc=1, device_id={"pairs": lax.rem(p + t, Z * K), "aux": w},
            device_id_type=pl.DeviceIdType.MESH)

    loop(1, CHIPS, plane_peer)
    loop(1, Z * K, column_peer)


def met():
    pl.semaphore_wait(pltpu.get_barrier_semaphore(), CHIPS + Z * K - 2)


def loop(start, stop, body):
    def step(t, c):
        body(t)
        return c

    lax.fori_loop(start, stop, step, 0)


def split(x):
    hi = x.astype(BF16)
    return hi, (x - hi.astype(F32)).astype(BF16)


def dot(a, b):
    return lax.dot_general(a, b, (((1,), (0,)), ((), ())), preferred_element_type=F32)


def dot_t(a, b, precision=None):
    return lax.dot_general(a, b, (((1,), (1,)), ((), ())), preferred_element_type=F32, precision=precision)


def kernel(amp_hbm, fac, occ, out,
           amp, flip, slots, mine, sall, ball, s3, b3, y3, acc,
           sib, half, parts, tall, at, gb, slot_a, slot_b, hd, hr, occs, gm, cm, hs, hout,
           in_sem, ex_send, ex_recv, a_send, a_recv, s_send, s_recv, w_send, w_recv, l_send, ring_send, ring_recv,
           q_send, q_recv, h_send, h_recv, c_send, c_recv, r_send, r_recv, f_send, f_recv, g_send, g_recv):
    p = lax.axis_index("pairs")
    w = lax.axis_index("aux")
    z, k = p // K, lax.rem(p, K)
    core = lax.rem(k, 2)
    m = w * K + k
    chip = w * 2 + k // 2
    other = p + 1 - 2 * core
    virt = amp.shape[1]
    cols = virt // W
    local = ball.shape[0]
    half_of = k // 2

    load = pltpu.make_async_copy(amp_hbm, amp, in_sem)
    load.start()
    greet(p, w, z, core, chip)
    met()

    def mine_of(gi, kk):
        return fac.at[pl.ds(kk * ball.shape[0] + GROUPS[gi][0], GROUPS[gi][1])]

    def my_rows(gi):
        return ball.at[pl.ds(*GROUPS[gi]), pl.ds(pl.multiple_of(8 * p, 8), 8), :]

    def region(gi, part, origin):
        row = origin * 32 + (half_of if part == 0 else 1 - half_of) * 16
        return ball.at[pl.ds(*GROUPS[gi]), pl.ds(pl.multiple_of(row, 16), 16), :]

    def keep(gi):
        return pltpu.make_async_copy(mine_of(gi, k), my_rows(gi), ex_recv.at[gi, 0])

    def exchange(gi, t):
        kk = lax.rem(half_of + t // 2, 2) * 2 + lax.rem(core + t, 2)
        return remote(mine_of(gi, kk), my_rows(gi), ex_send.at[gi, t], ex_recv.at[gi, t // 2], z * K + kk, w)

    def neighbour(way):
        return lax.rem(z + (1 if way == 0 else Z - 1), Z) * K

    def hops(way, gi, part):
        return 4 - (way + gi + part) % 2

    def launch(way, gi, t):
        kk = half_of * 2 + lax.rem(core + t, 2)
        return remote(mine_of(gi, kk), my_rows(gi), l_send.at[way, gi, t], ring_recv.at[way, gi, 0, 0],
                      neighbour(way) + kk, w)

    def ring(way, gi, part, h):
        here = region(gi, part, lax.rem(z + (Z - h if way == 0 else h), Z))
        return remote(here, here, ring_send.at[way, gi, part, h], ring_recv.at[way, gi, part, h],
                      neighbour(way) + k, w)

    def arrive(way, gi, part, h):
        here = region(gi, part, lax.rem(z + (Z - 1 - h if way == 0 else 1 + h), Z))
        remote(here, here, ring_send.at[way, gi, part, h], ring_recv.at[way, gi, part, h],
               neighbour(way) + k, w).wait_recv()

    def begin(gi):
        for way in range(2):
            for t in range(2):
                launch(way, gi, t).start()
        keep(gi).start()
        for t in range(1, K):
            exchange(gi, t).start()

    def begin_far(gi):
        wait_bytes(region(gi, 1, z), ex_recv.at[gi, 1])
        for way in range(2):
            ring(way, gi, 1, 0).start()

    def forward(gi, part, h):
        for way in range(2):
            if h < hops(way, gi, part):
                arrive(way, gi, part, h - 1)
                ring(way, gi, part, h).start()

    def landed(h):
        for gi in range(2):
            for part in range(2):
                for way in range(2):
                    if hops(way, gi, part) == h + 1:
                        arrive(way, gi, part, h)

    begin(0)
    begin(1)

    def straight(t):
        kk = lax.rem(k + t, K)
        src = amp.at[:, pl.ds(pl.multiple_of((w * K + kk) * 8, 8), 8), :]
        dst = slots.at[pl.ds(2 * k, 2)]
        if t == 0:
            return pltpu.make_async_copy(src, dst, a_recv)
        return remote(src, dst, a_send, a_recv, z * K + kk, w)

    def turned_far(s, kk):
        src = flip.at[s, pl.ds(pl.multiple_of((w * K + kk) * 8, 8), 8), :]
        return remote(src, slots.at[Z + z], a_send, a_recv, (2 * k + s) * K + kk, w)

    def turned_near(s, kk):
        src = flip.at[s, pl.ds(pl.multiple_of((w * K + kk) * 8, 8), 8), :]
        return pltpu.make_async_copy(src, slots.at[Z + z], a_recv)

    load.wait()
    for s in range(2):
        flip[s] = amp[s].T
    for s in range(2):
        for kk in range(K):
            here = jnp.logical_and(2 * k + s == z, kk == k)
            pl.when(here)(lambda s=s, kk=kk: turned_near(s, kk).start())
            pl.when(jnp.logical_not(here))(lambda s=s, kk=kk: turned_far(s, kk).start())
    for t in range(K):
        straight(t).start()
    begin_far(0)
    begin_far(1)

    def share(t):
        n = lax.rem(chip + t, CHIPS)
        return remote(mine, sall.at[:, chip, core], s_send, s_recv, z * K + lax.rem(n, 2) * 2 + core, n // 2)

    wait_bytes(slots, a_recv)
    for d in range(OFFSETS):
        j = lax.rem(z + d, Z)
        mine[d] = slots[j] + slots[Z + j]
    pltpu.make_async_copy(mine, sall.at[:, chip, core], s_recv).start()
    loop(1, CHIPS, lambda t: share(t).start())
    for part in range(2):
        for gi in range(2):
            forward(gi, part, 1)

    def occ_share(t):
        return remote(occ, occs.at[w], q_send, q_recv, p, lax.rem(w + t, W))

    pltpu.make_async_copy(occ, occs.at[w], q_recv).start()
    loop(1, W, lambda t: occ_share(t).start())
    at_w = pl.ds(pl.multiple_of(w * cols, cols), cols)
    for s in range(2):
        hd[:, s * cols:(s + 1) * cols] = flip[s, at_w, :].T
        hd[:, (2 + s) * cols:(3 + s) * cols] = amp[s, at_w, :].T
    forward(0, 0, 2)
    forward(1, 0, 2)
    wait_bytes(sall.at[:, :, core], s_recv)
    across = remote(sall.at[:, :, core], sall.at[:, :, core], w_send, w_recv, other, w)
    across.start()
    forward(0, 1, 2)
    forward(1, 1, 2)

    wait_bytes(occs, q_recv)
    g_sum = dot_t(occs[0], occs[0], highest)
    for n in range(1, W):
        g_sum = g_sum + dot_t(occs[n], occs[n], highest)
    gm[...] = g_sum
    by_k = [gm[pl.ds(kk, 8, stride=8), :] for kk in range(8)]
    for j in range(8):
        cm[pl.ds(j, 8, stride=8), :] = jnp.concatenate([x[:, j * 8:j * 8 + 8] for x in by_k], axis=1)

    wait_bytes(sall.at[:, :, 1 - core], w_recv)
    for d in range(OFFSETS):
        hi, lo = split(sall[d].reshape(virt, virt))
        s3[d, :virt], s3[d, virt:2 * virt], s3[d, 2 * virt:] = hi, lo, hi

    def first(origin):
        rows = pl.ds(pl.multiple_of(origin * 32, 32), 32)
        hi, lo = split(ball[:, rows, :])
        b3[:, rows, :virt], b3[:, rows, virt:2 * virt], b3[:, rows, 2 * virt:] = hi, hi, lo

        def one(d):
            y_hi, y_lo = split(dot(b3[:, rows, :].reshape(local * 32, 3 * virt), s3[d]))
            for q in range(local):
                at_q = q * 3 * virt
                y3[d, rows, at_q:at_q + virt] = y_hi[q * 32:(q + 1) * 32]
                y3[d, rows, at_q + virt:at_q + 2 * virt] = y_lo[q * 32:(q + 1) * 32]
                y3[d, rows, at_q + 2 * virt:at_q + 3 * virt] = y_hi[q * 32:(q + 1) * 32]

        loop(0, OFFSETS, one)

    def both(step):
        loop(0, 2, lambda t: first(lax.rem(z + step + t * (Z - 2 * step), Z)))

    def second(d):
        term = None
        for q in range(local):
            x = dot_t(y3[d, :, q * 3 * virt:(q + 1) * 3 * virt], b3[q])
            term = x if term is None else term + x
        acc[pl.ds(pl.multiple_of(d * virt, virt), virt)] = term

    sums = acc.reshape(OFFSETS, CHIPS, 2, 8, virt)

    def swap(d):
        return remote(sums.at[d, :, 1 - core], sib.at[d], c_send.at[d], c_recv.at[d], other, w)

    for gi in range(2):
        wait_bytes(region(gi, 0, z), ex_recv.at[gi, 0])
    first(z)
    forward(0, 0, 3)
    both(1)
    forward(1, 0, 3)
    both(2)
    forward(0, 1, 3)
    forward(1, 1, 3)
    landed(2)
    both(3)
    landed(3)
    first(lax.rem(z + 4, Z))

    def hole_send(t):
        q = lax.rem(p + t, Z * K)
        return remote(hd.at[pl.ds(pl.multiple_of(q * 8, 8), 8), :], hr.at[p], h_send, h_recv, q, w)

    groups = ((0, 3), (3, 5))

    def spread(t, e):
        n = lax.rem(chip + t, CHIPS)
        ds = pl.ds(groups[e][0], groups[e][1] - groups[e][0])
        return remote(half.at[ds, n], parts.at[chip, ds], r_send, r_recv, z * K + lax.rem(n, 2) * 2 + core, n // 2)

    def spread_group(e):
        low, high = groups[e]
        for d in range(low, high):
            swap(d).wait_recv()
            half[d] = sums[d, :, core] + sib[d]
        ds = pl.ds(low, high - low)
        pltpu.make_async_copy(half.at[ds, chip], parts.at[chip, ds], r_recv).start()
        loop(1, CHIPS, lambda t: spread(t, e).start())

    def finish(d):
        second(d)
        swap(d).start()
        pl.when(d == groups[0][1])(lambda: spread_group(0))

    loop(0, OFFSETS, finish)
    pltpu.make_async_copy(hd.at[pl.ds(pl.multiple_of(p * 8, 8), 8), :], hr.at[p], h_recv).start()
    spread_group(1)
    loop(1, Z * K, lambda t: hole_send(t).start())

    wait_bytes(hr, h_recv)
    flat = hr.reshape(Z * K * 8, 4 * cols)
    by_a = [flat[pl.ds(a, Z * K, stride=8), :] for a in range(8)]
    for s in range(2):
        for e in range(2):
            hs[e, pl.ds(s, Z * K, stride=2), :] = jnp.concatenate(
                [x[:, s * cols:(s + 1) * cols] for x in by_a[4 * e:4 * e + 4]], axis=1)
    for l2 in range(4):
        by_a = [flat[pl.ds(8 * l2 + a, 8, stride=32), :] for a in range(8)]
        for s in range(2):
            for e in range(2):
                at_row = 16 * l2 + 8 * s
                hs[e, at_row:at_row + 8, :] += jnp.concatenate(
                    [x[:, (2 + s) * cols:(3 + s) * cols] for x in by_a[4 * e:4 * e + 4]], axis=1)
    hole = [lax.dot_general(cm[...], hs[e], (((1,), (0,)), ((), ())), preferred_element_type=F32, precision=highest)
            for e in range(2)]
    for a in range(8):
        hout[pl.ds(a, 64, stride=8), :] = hole[a // 4][:, a % 4 * cols:(a % 4 + 1) * cols]

    wait_bytes(parts, r_recv)
    total = parts[0]
    for n in range(1, CHIPS):
        total = total + parts[n]
    tall[...] = jnp.zeros_like(tall)
    for d in range(4):
        tall[pl.ds(pl.multiple_of(d * 32 + 8 * k, 8), 8), :] = total[d]
    at[...] = tall[...].T
    for ww in range(W):
        for d in range(1, OFFSETS):
            gb[ww, :, (d - 1) * cols:d * cols] = total[d][:, ww * cols:(ww + 1) * cols]

    def col_send(t):
        q = lax.rem(p + t, Z * K)
        return remote(at.at[pl.ds(pl.multiple_of(q * 8, 8), 8), :], slot_a.at[p], f_send, f_recv, q, w)

    def row_send(ww):
        return remote(gb.at[ww], slot_b.at[z], g_send, g_recv, m, ww)

    def row_here(ww):
        return jnp.logical_and(m == p, ww == w)

    for ww in range(W):
        pl.when(row_here(ww))(lambda ww=ww: pltpu.make_async_copy(gb.at[ww], slot_b.at[z], g_recv).start())
        pl.when(jnp.logical_not(row_here(ww)))(lambda ww=ww: row_send(ww).start())
    pltpu.make_async_copy(at.at[pl.ds(pl.multiple_of(p * 8, 8), 8), :], slot_a.at[p], f_recv).start()
    loop(1, Z * K, lambda t: col_send(t).start())

    wait_bytes(slot_b, g_recv)
    for zz in range(Z):
        tile = slot_b[zz]
        for d in range(1, OFFSETS):
            pair = zz * 8 + (zz + d) % 8
            out[pair] = tile[:, (d - 1) * cols:d * cols] + hout[pair * 8:pair * 8 + 8, :]
    wait_bytes(slot_a, f_recv)
    for zz in range(Z):
        tile = slot_a[zz * K] + slot_a[zz * K + 1] + slot_a[zz * K + 2] + slot_a[zz * K + 3]
        for d in range(4):
            pair = (zz + d) % 8 * 8 + zz
            out[pair] = tile[:, d * cols:(d + 1) * cols] + hout[pair * 8:pair * 8 + 8, :]

    for gi in range(len(GROUPS)):
        for t in range(1, K):
            exchange(gi, t).wait_send()
        for way in range(2):
            for t in range(2):
                launch(way, gi, t).wait_send()
            for part in range(2):
                for h in range(1 - part, hops(way, gi, part)):
                    ring(way, gi, part, h).wait_send()
    for t in range(1, K):
        straight(t).wait_send()
    for s in range(2):
        for kk in range(K):
            here = jnp.logical_and(2 * k + s == z, kk == k)
            pl.when(jnp.logical_not(here))(lambda s=s, kk=kk: turned_far(s, kk).wait_send())
    across.wait_send()
    for d in range(OFFSETS):
        swap(d).wait_send()
    for ww in range(W):
        pl.when(jnp.logical_not(row_here(ww)))(lambda ww=ww: row_send(ww).wait_send())
    wait_bytes(parts.at[pl.ds(0, CHIPS - 1)], s_send)
    wait_bytes(parts.at[pl.ds(0, CHIPS - 1)], r_send)
    wait_bytes(occs.at[pl.ds(0, W - 1)], q_send)
    wait_bytes(hr.at[pl.ds(0, Z * K - 1)], h_send)
    wait_bytes(slot_a.at[pl.ds(0, Z * K - 1)], f_send)


def shards(amplitudes, factors, occ_factors):
    aux_local, rows, virt = factors.shape
    occupied = occ_factors.shape[1]
    local = aux_local // K
    cols = virt // W
    occ = occ_factors.transpose(1, 2, 0).reshape(occupied * occupied, aux_local)
    vm = pl.BlockSpec(memory_space=pltpu.VMEM)
    anywhere = pl.BlockSpec(memory_space=pltpu.HBM)
    dma = pltpu.SemaphoreType.DMA
    v = pltpu.VMEM
    scratch = [
        v((2, virt, virt), F32), v((2, virt, virt), F32),
        v((2 * Z, 8, virt), F32), v((OFFSETS, 8, virt), F32),
        v((OFFSETS, CHIPS, 2, 8, virt), F32), v((local, virt, virt), F32),
        v((OFFSETS, 3 * virt, virt), BF16), v((local, virt, 3 * virt), BF16),
        v((OFFSETS, virt, local * 3 * virt), BF16),
        v((OFFSETS * virt, virt), F32),
        v((OFFSETS, CHIPS, 8, virt), F32), v((OFFSETS, CHIPS, 8, virt), F32),
        v((CHIPS, OFFSETS, 8, virt), F32),
        v((128, virt), F32), v((virt, 128), F32),
        v((W, 8, 128), F32), v((Z * K, 8, 128), F32), v((Z, 8, 128), F32),
        v((virt, 128), F32), v((Z * K, 8, 128), F32),
        v((W, occupied * occupied, aux_local), F32),
        v((64, 64), F32), v((64, 64), F32), v((2, 64, 128), F32), v((64 * 8, cols), F32),
        dma(()), dma((len(GROUPS), K)), dma((len(GROUPS), 2)),
        dma(()), dma(()), dma(()), dma(()), dma(()), dma(()),
        dma((2, len(GROUPS), 2)), dma((2, len(GROUPS), 2, 4)), dma((2, len(GROUPS), 2, 4)),
        dma(()), dma(()), dma(()), dma(()), dma((OFFSETS,)), dma((OFFSETS,)), dma(()), dma(()), dma(()), dma(()), dma(()), dma(()),
    ]
    return pl.pallas_call(
        kernel,
        out_shape=jax.ShapeDtypeStruct((occupied * occupied, rows, cols), F32),
        in_specs=[anywhere, anywhere, vm],
        out_specs=vm,
        scratch_shapes=scratch,
        compiler_params=pltpu.CompilerParams(
            collective_id=0, has_side_effects=True, vmem_limit_bytes=(64 << 20) - (330 << 10)),
        name="residual",
    )(amplitudes, factors, occ)


def solution(mesh):
    placed = (P("pairs", None, None), P("aux", "pairs", None), P("aux", None, None))
    return jax.shard_map(
        shards, mesh=mesh, in_specs=placed, out_specs=P(None, "pairs", "aux"), check_vma=False
    )
```

```python
import jax
import jax.numpy as jnp
from jax import lax
from jax.experimental import pallas as pl
from jax.experimental.pallas import tpu as pltpu
from jax.sharding import PartitionSpec as P

highest = lax.Precision.HIGHEST
F32 = jnp.float32
BF16 = jnp.bfloat16

Z = 8
K = 4
W = 8
PLANE = K * W
CHIPS = PLANE // 2
OFFSETS = 5
GROUPS = ((0, 6), (6, 6))


SUMS = ((0, 2), (2, 4), (4, 5))


def remote(src, dst, send_sem, recv_sem, p, w):
    return pltpu.make_async_remote_copy(
        src_ref=src,
        dst_ref=dst,
        send_sem=send_sem,
        recv_sem=recv_sem,
        device_id={"pairs": p, "aux": w},
        device_id_type=pl.DeviceIdType.MESH,
    )


def wait_bytes(ref, sem):
    pltpu.make_async_copy(ref, ref, sem).wait()


def greet(p, w, z, core, chip):
    barrier = pltpu.get_barrier_semaphore()

    def plane_peer(t):
        n = lax.rem(chip + t, CHIPS)
        pl.semaphore_signal(
            barrier, inc=1, device_id={"pairs": z * K + lax.rem(n, 2) * 2 + core, "aux": n // 2},
            device_id_type=pl.DeviceIdType.MESH)

    def column_peer(t):
        pl.semaphore_signal(
            barrier, inc=1, device_id={"pairs": lax.rem(p + t, Z * K), "aux": w},
            device_id_type=pl.DeviceIdType.MESH)

    loop(1, CHIPS, plane_peer)
    loop(1, Z * K, column_peer)


def met():
    pl.semaphore_wait(pltpu.get_barrier_semaphore(), CHIPS + Z * K - 2)


def loop(start, stop, body):
    def step(t, c):
        body(t)
        return c

    lax.fori_loop(start, stop, step, 0)


def split(x):
    hi = x.astype(BF16)
    return hi, (x - hi.astype(F32)).astype(BF16)


def dot(a, b):
    return lax.dot_general(a, b, (((1,), (0,)), ((), ())), preferred_element_type=F32)


def dot_t(a, b, precision=None):
    return lax.dot_general(a, b, (((1,), (1,)), ((), ())), preferred_element_type=F32, precision=precision)


def kernel(amp_hbm, fac, occ, out,
           amp, flip, slots, mine, sall, ball, s3, b3, y3, acc,
           sib, half, parts, tall, at, gb, gb4, slot_a, slot_b, slot_b4, hd, hr, occs, gm, cm, hs, hout,
           in_sem, ex_send, ex_recv, a_send, a_recv, s_send, s_recv, w_send, w_recv, l_send, ring_send, ring_recv,
           q_send, q_recv, h_send, h_recv, c_send, c_recv, r_send, r_recv, f_send, f_recv, g_send, g_recv):
    p = lax.axis_index("pairs")
    w = lax.axis_index("aux")
    z, k = p // K, lax.rem(p, K)
    core = lax.rem(k, 2)
    m = w * K + k
    chip = w * 2 + k // 2
    other = p + 1 - 2 * core
    virt = amp.shape[1]
    cols = virt // W
    local = ball.shape[0]
    half_of = k // 2

    load = pltpu.make_async_copy(amp_hbm, amp, in_sem)
    load.start()
    greet(p, w, z, core, chip)
    met()

    def mine_of(gi, kk):
        return fac.at[pl.ds(kk * ball.shape[0] + GROUPS[gi][0], GROUPS[gi][1])]

    def my_rows(gi):
        return ball.at[pl.ds(*GROUPS[gi]), pl.ds(pl.multiple_of(8 * p, 8), 8), :]

    def region(gi, part, origin):
        row = origin * 32 + (half_of if part == 0 else 1 - half_of) * 16
        return ball.at[pl.ds(*GROUPS[gi]), pl.ds(pl.multiple_of(row, 16), 16), :]

    def keep(gi):
        return pltpu.make_async_copy(mine_of(gi, k), my_rows(gi), ex_recv.at[gi, 0])

    def exchange(gi, t):
        kk = lax.rem(half_of + t // 2, 2) * 2 + lax.rem(core + t, 2)
        return remote(mine_of(gi, kk), my_rows(gi), ex_send.at[gi, t], ex_recv.at[gi, t // 2], z * K + kk, w)

    def neighbour(way):
        return lax.rem(z + (1 if way == 0 else Z - 1), Z) * K

    def hops(way, gi, part):
        return 4 - (way + gi + part) % 2

    def launch(way, gi, t):
        kk = half_of * 2 + lax.rem(core + t, 2)
        return remote(mine_of(gi, kk), my_rows(gi), l_send.at[way, gi, t], ring_recv.at[way, gi, 0, 0],
                      neighbour(way) + kk, w)

    def ring(way, gi, part, h):
        here = region(gi, part, lax.rem(z + (Z - h if way == 0 else h), Z))
        return remote(here, here, ring_send.at[way, gi, part, h], ring_recv.at[way, gi, part, h],
                      neighbour(way) + k, w)

    def arrive(way, gi, part, h):
        here = region(gi, part, lax.rem(z + (Z - 1 - h if way == 0 else 1 + h), Z))
        remote(here, here, ring_send.at[way, gi, part, h], ring_recv.at[way, gi, part, h],
               neighbour(way) + k, w).wait_recv()

    def begin(gi):
        for way in range(2):
            for t in range(2):
                launch(way, gi, t).start()
        keep(gi).start()
        for t in range(1, K):
            exchange(gi, t).start()

    def begin_far(gi):
        wait_bytes(region(gi, 1, z), ex_recv.at[gi, 1])
        for way in range(2):
            ring(way, gi, 1, 0).start()

    def forward(gi, part, h):
        for way in range(2):
            if h < hops(way, gi, part):
                arrive(way, gi, part, h - 1)
                ring(way, gi, part, h).start()

    def landed(h):
        for gi in range(len(GROUPS)):
            for part in range(2):
                for way in range(2):
                    if hops(way, gi, part) == h + 1:
                        arrive(way, gi, part, h)

    for gi in range(len(GROUPS)):
        begin(gi)

    def straight(t):
        kk = lax.rem(k + t, K)
        src = amp.at[:, pl.ds(pl.multiple_of((w * K + kk) * 8, 8), 8), :]
        dst = slots.at[pl.ds(2 * k, 2)]
        if t == 0:
            return pltpu.make_async_copy(src, dst, a_recv)
        return remote(src, dst, a_send, a_recv, z * K + kk, w)

    def turned_far(s, kk):
        src = flip.at[s, pl.ds(pl.multiple_of((w * K + kk) * 8, 8), 8), :]
        return remote(src, slots.at[Z + z], a_send, a_recv, (2 * k + s) * K + kk, w)

    def turned_near(s, kk):
        src = flip.at[s, pl.ds(pl.multiple_of((w * K + kk) * 8, 8), 8), :]
        return pltpu.make_async_copy(src, slots.at[Z + z], a_recv)

    load.wait()
    for s in range(2):
        flip[s] = amp[s].T
    for s in range(2):
        for kk in range(K):
            here = jnp.logical_and(2 * k + s == z, kk == k)
            pl.when(here)(lambda s=s, kk=kk: turned_near(s, kk).start())
            pl.when(jnp.logical_not(here))(lambda s=s, kk=kk: turned_far(s, kk).start())
    for t in range(K):
        straight(t).start()
    for gi in range(len(GROUPS)):
        begin_far(gi)

    def share(t):
        n = lax.rem(chip + t, CHIPS)
        return remote(mine, sall.at[:, chip, core], s_send, s_recv, z * K + lax.rem(n, 2) * 2 + core, n // 2)

    wait_bytes(slots, a_recv)
    for d in range(OFFSETS):
        j = lax.rem(z + d, Z)
        mine[d] = slots[j] + slots[Z + j]
    pltpu.make_async_copy(mine, sall.at[:, chip, core], s_recv).start()
    loop(1, CHIPS, lambda t: share(t).start())
    for part in range(2):
        for gi in range(len(GROUPS)):
            forward(gi, part, 1)

    def occ_share(t):
        return remote(occ, occs.at[w], q_send, q_recv, p, lax.rem(w + t, W))

    pltpu.make_async_copy(occ, occs.at[w], q_recv).start()
    loop(1, W, lambda t: occ_share(t).start())
    at_w = pl.ds(pl.multiple_of(w * cols, cols), cols)
    for s in range(2):
        hd[:, s * cols:(s + 1) * cols] = flip[s, at_w, :].T
        hd[:, (2 + s) * cols:(3 + s) * cols] = amp[s, at_w, :].T
    for gi in range(len(GROUPS)):
        forward(gi, 0, 2)
    wait_bytes(sall.at[:, :, core], s_recv)
    across = remote(sall.at[:, :, core], sall.at[:, :, core], w_send, w_recv, other, w)
    across.start()
    for gi in range(len(GROUPS)):
        forward(gi, 1, 2)

    wait_bytes(occs, q_recv)
    g_sum = dot_t(occs[0], occs[0], highest)
    for n in range(1, W):
        g_sum = g_sum + dot_t(occs[n], occs[n], highest)
    gm[...] = g_sum
    by_k = [gm[pl.ds(kk, 8, stride=8), :] for kk in range(8)]
    for j in range(8):
        cm[pl.ds(j, 8, stride=8), :] = jnp.concatenate([x[:, j * 8:j * 8 + 8] for x in by_k], axis=1)

    wait_bytes(sall.at[:, :, 1 - core], w_recv)
    for d in range(OFFSETS):
        hi, lo = split(sall[d].reshape(virt, virt))
        s3[d, :virt], s3[d, virt:2 * virt], s3[d, 2 * virt:] = hi, lo, hi

    def first(origin):
        rows = pl.ds(pl.multiple_of(origin * 32, 32), 32)
        hi, lo = split(ball[:, rows, :])
        b3[:, rows, :virt], b3[:, rows, virt:2 * virt], b3[:, rows, 2 * virt:] = hi, hi, lo

        def one(d):
            y_hi, y_lo = split(dot(b3[:, rows, :].reshape(local * 32, 3 * virt), s3[d]))
            for q in range(local):
                at_q = q * 3 * virt
                y3[d, rows, at_q:at_q + virt] = y_hi[q * 32:(q + 1) * 32]
                y3[d, rows, at_q + virt:at_q + 2 * virt] = y_lo[q * 32:(q + 1) * 32]
                y3[d, rows, at_q + 2 * virt:at_q + 3 * virt] = y_hi[q * 32:(q + 1) * 32]

        loop(0, OFFSETS, one)

    def both(step):
        loop(0, 2, lambda t: first(lax.rem(z + step + t * (Z - 2 * step), Z)))

    def second(d):
        term = None
        for q in range(local):
            x = dot_t(y3[d, :, q * 3 * virt:(q + 1) * 3 * virt], b3[q])
            term = x if term is None else term + x
        acc[pl.ds(pl.multiple_of(d * virt, virt), virt)] = term

    sums = acc.reshape(OFFSETS, CHIPS, 2, 8, virt)

    def swap(d):
        return remote(sums.at[d, :, 1 - core], sib.at[d], c_send.at[d], c_recv.at[d], other, w)

    for gi in range(len(GROUPS)):
        wait_bytes(region(gi, 0, z), ex_recv.at[gi, 0])
    first(z)
    late = [(gi, part) for part in range(2) for gi in range(len(GROUPS))]
    share_of = len(late) // 4
    for gi, part in late[:share_of]:
        forward(gi, part, 3)
    both(1)
    for gi, part in late[share_of:2 * share_of]:
        forward(gi, part, 3)
    both(2)
    for gi, part in late[2 * share_of:]:
        forward(gi, part, 3)
    def hole_send(t):
        q = lax.rem(p + t, Z * K)
        return remote(hd.at[pl.ds(pl.multiple_of(q * 8, 8), 8), :], hr.at[p], h_send, h_recv, q, w)

    pltpu.make_async_copy(hd.at[pl.ds(pl.multiple_of(p * 8, 8), 8), :], hr.at[p], h_recv).start()
    loop(1, Z * K, lambda t: hole_send(t).start())
    landed(2)
    both(3)
    landed(3)
    first(lax.rem(z + 4, Z))


    def spread(t, e):
        n = lax.rem(chip + t, CHIPS)
        ds = pl.ds(SUMS[e][0], SUMS[e][1] - SUMS[e][0])
        return remote(half.at[ds, n], parts.at[chip, ds], r_send, r_recv.at[e], z * K + lax.rem(n, 2) * 2 + core, n // 2)

    def spread_group(e):
        low, high = SUMS[e]
        for d in range(low, high):
            swap(d).wait_recv()
            half[d] = sums[d, :, core] + sib[d]
        ds = pl.ds(low, high - low)
        pltpu.make_async_copy(half.at[ds, chip], parts.at[chip, ds], r_recv.at[e]).start()
        loop(1, CHIPS, lambda t: spread(t, e).start())

    def finish(d):
        second(d)
        swap(d).start()
        for e in range(len(SUMS) - 1):
            pl.when(d == SUMS[e][1])(lambda e=e: spread_group(e))

    loop(0, OFFSETS, finish)
    wait_bytes(hr, h_recv)
    flat = hr.reshape(Z * K * 8, 4 * cols)
    by_a = [flat[pl.ds(a, Z * K, stride=8), :] for a in range(8)]
    for s in range(2):
        for e in range(2):
            hs[e, pl.ds(s, Z * K, stride=2), :] = jnp.concatenate(
                [x[:, s * cols:(s + 1) * cols] for x in by_a[4 * e:4 * e + 4]], axis=1)
    for l2 in range(4):
        by_a = [flat[pl.ds(8 * l2 + a, 8, stride=32), :] for a in range(8)]
        for s in range(2):
            for e in range(2):
                at_row = 16 * l2 + 8 * s
                hs[e, at_row:at_row + 8, :] += jnp.concatenate(
                    [x[:, (2 + s) * cols:(3 + s) * cols] for x in by_a[4 * e:4 * e + 4]], axis=1)
    hole = [lax.dot_general(cm[...], hs[e], (((1,), (0,)), ((), ())), preferred_element_type=F32, precision=highest)
            for e in range(2)]
    for a in range(8):
        hout[pl.ds(a, 64, stride=8), :] = hole[a // 4][:, a % 4 * cols:(a % 4 + 1) * cols]
    spread_group(len(SUMS) - 1)

    for gi in range(len(GROUPS)):
        for t in range(1, K):
            exchange(gi, t).wait_send()
        for way in range(2):
            for t in range(2):
                launch(way, gi, t).wait_send()
            for part in range(2):
                for h in range(1 - part, hops(way, gi, part)):
                    ring(way, gi, part, h).wait_send()
    for t in range(1, K):
        straight(t).wait_send()
    for s in range(2):
        for kk in range(K):
            here = jnp.logical_and(2 * k + s == z, kk == k)
            pl.when(jnp.logical_not(here))(lambda s=s, kk=kk: turned_far(s, kk).wait_send())
    across.wait_send()
    for d in range(OFFSETS):
        swap(d).wait_send()
    wait_bytes(parts.at[pl.ds(0, CHIPS - 1)], s_send)
    wait_bytes(parts.at[pl.ds(0, CHIPS - 1)], r_send)
    wait_bytes(occs.at[pl.ds(0, W - 1)], q_send)
    wait_bytes(hr.at[pl.ds(0, Z * K - 1)], h_send)

    def gathered(e):
        low, high = SUMS[e]
        ds = pl.ds(low, high - low)
        wait_bytes(parts.at[:, ds], r_recv.at[e])
        total = parts[0, low:high]
        for n in range(1, CHIPS):
            total = total + parts[n, low:high]
        return [total[n] for n in range(high - low)]

    def col_send(t):
        q = lax.rem(p + t, Z * K)
        return remote(at.at[pl.ds(pl.multiple_of(q * 8, 8), 8), :], slot_a.at[p], f_send, f_recv, q, w)

    def row_send(e, ww):
        src, dst = ((gb, slot_b), (gb4, slot_b4))[e]
        return remote(src.at[ww], dst.at[z], g_send.at[e], g_recv.at[e], m, ww)

    def row_keep(e, ww):
        src, dst = ((gb, slot_b), (gb4, slot_b4))[e]
        return pltpu.make_async_copy(src.at[ww], dst.at[z], g_recv.at[e])

    def rows_start(e):
        for ww in range(W):
            here = jnp.logical_and(m == p, ww == w)
            pl.when(here)(lambda ww=ww: row_keep(e, ww).start())
            pl.when(jnp.logical_not(here))(lambda ww=ww: row_send(e, ww).start())

    def rows_sent(e):
        for ww in range(W):
            here = jnp.logical_and(m == p, ww == w)
            pl.when(jnp.logical_not(here))(lambda ww=ww: row_send(e, ww).wait_send())

    tall[...] = jnp.zeros_like(tall)
    total = sum([gathered(e) for e in range(len(SUMS) - 1)], [])
    for d in range(4):
        tall[pl.ds(pl.multiple_of(d * 32 + 8 * k, 8), 8), :] = total[d]
    for ww in range(W):
        for d in range(1, 4):
            gb[ww, :, (d - 1) * cols:d * cols] = total[d][:, ww * cols:(ww + 1) * cols]
    at[...] = tall[...].T
    pltpu.make_async_copy(at.at[pl.ds(pl.multiple_of(p * 8, 8), 8), :], slot_a.at[p], f_recv).start()
    loop(1, Z * K, lambda t: col_send(t).start())
    rows_start(0)
    last, = gathered(len(SUMS) - 1)
    for ww in range(W):
        gb4[ww] = last[:, ww * cols:(ww + 1) * cols]
    rows_start(1)

    def result(pair, value):
        out[pair] = value + hout[pair * 8:pair * 8 + 8, :]

    wait_bytes(slot_a, f_recv)
    for zz in range(Z):
        tile = slot_a[zz * K] + slot_a[zz * K + 1] + slot_a[zz * K + 2] + slot_a[zz * K + 3]
        for d in range(4):
            result((zz + d) % 8 * 8 + zz, tile[:, d * cols:(d + 1) * cols])
    wait_bytes(slot_b, g_recv.at[0])
    for zz in range(Z):
        tile = slot_b[zz]
        for d in range(1, 4):
            result(zz * 8 + (zz + d) % 8, tile[:, (d - 1) * cols:d * cols])
    wait_bytes(slot_a.at[pl.ds(0, Z * K - 1)], f_send)
    rows_sent(0)
    wait_bytes(slot_b4, g_recv.at[1])
    for zz in range(Z):
        result(zz * 8 + (zz + 4) % 8, slot_b4[zz])
    rows_sent(1)


def shards(amplitudes, factors, occ_factors):
    aux_local, rows, virt = factors.shape
    occupied = occ_factors.shape[1]
    local = aux_local // K
    cols = virt // W
    occ = occ_factors.transpose(1, 2, 0).reshape(occupied * occupied, aux_local)
    vm = pl.BlockSpec(memory_space=pltpu.VMEM)
    anywhere = pl.BlockSpec(memory_space=pltpu.HBM)
    dma = pltpu.SemaphoreType.DMA
    v = pltpu.VMEM
    scratch = [
        v((2, virt, virt), F32), v((2, virt, virt), F32),
        v((2 * Z, 8, virt), F32), v((OFFSETS, 8, virt), F32),
        v((OFFSETS, CHIPS, 2, 8, virt), F32), v((local, virt, virt), F32),
        v((OFFSETS, 3 * virt, virt), BF16), v((local, virt, 3 * virt), BF16),
        v((OFFSETS, virt, local * 3 * virt), BF16),
        v((OFFSETS * virt, virt), F32),
        v((OFFSETS, CHIPS, 8, virt), F32), v((OFFSETS, CHIPS, 8, virt), F32),
        v((CHIPS, OFFSETS, 8, virt), F32),
        v((128, virt), F32), v((virt, 128), F32),
        v((W, 8, 3 * cols), F32), v((W, 8, cols), F32),
        v((Z * K, 8, 128), F32), v((Z, 8, 3 * cols), F32), v((Z, 8, cols), F32),
        v((virt, 128), F32), v((Z * K, 8, 128), F32),
        v((W, occupied * occupied, aux_local), F32),
        v((64, 64), F32), v((64, 64), F32), v((2, 64, 128), F32), v((64 * 8, cols), F32),
        dma(()), dma((len(GROUPS), K)), dma((len(GROUPS), 2)),
        dma(()), dma(()), dma(()), dma(()), dma(()), dma(()),
        dma((2, len(GROUPS), 2)), dma((2, len(GROUPS), 2, 4)), dma((2, len(GROUPS), 2, 4)),
        dma(()), dma(()), dma(()), dma(()), dma((OFFSETS,)), dma((OFFSETS,)), dma(()), dma((len(SUMS),)), dma(()), dma(()), dma((2,)), dma((2,)),
    ]
    return pl.pallas_call(
        kernel,
        out_shape=jax.ShapeDtypeStruct((occupied * occupied, rows, cols), F32),
        in_specs=[anywhere, anywhere, vm],
        out_specs=vm,
        scratch_shapes=scratch,
        compiler_params=pltpu.CompilerParams(
            collective_id=0, has_side_effects=True, vmem_limit_bytes=48 << 20),
        name="residual",
    )(pltpu.with_memory_space_constraint(amplitudes, pltpu.HBM), pltpu.with_memory_space_constraint(factors, pltpu.HBM), occ)


def solution(mesh):
    placed = (P("pairs", None, None), P("aux", "pairs", None), P("aux", None, None))
    return jax.shard_map(
        shards, mesh=mesh, in_specs=placed, out_specs=P(None, "pairs", "aux"), check_vma=False
    )
```

```python
import jax
import jax.numpy as jnp
from jax import lax
from jax.experimental import pallas as pl
from jax.experimental.pallas import tpu as pltpu
from jax.sharding import PartitionSpec as P

highest = lax.Precision.HIGHEST
F32 = jnp.float32
BF16 = jnp.bfloat16

Z = 8
K = 4
W = 8
PLANE = K * W
CHIPS = PLANE // 2
OFFSETS = 5
GROUPS = ((0, 6), (6, 6))


SUMS = ((0, 2), (2, 4), (4, 5))


def remote(src, dst, send_sem, recv_sem, p, w):
    return pltpu.make_async_remote_copy(
        src_ref=src,
        dst_ref=dst,
        send_sem=send_sem,
        recv_sem=recv_sem,
        device_id={"pairs": p, "aux": w},
        device_id_type=pl.DeviceIdType.MESH,
    )


def wait_bytes(ref, sem):
    pltpu.make_async_copy(ref, ref, sem).wait()


def greet(p, w, z, core, chip):
    barrier = pltpu.get_barrier_semaphore()

    def plane_peer(t):
        n = lax.rem(chip + t, CHIPS)
        pl.semaphore_signal(
            barrier, inc=1, device_id={"pairs": z * K + lax.rem(n, 2) * 2 + core, "aux": n // 2},
            device_id_type=pl.DeviceIdType.MESH)

    def column_peer(t):
        pl.semaphore_signal(
            barrier, inc=1, device_id={"pairs": lax.rem(p + t, Z * K), "aux": w},
            device_id_type=pl.DeviceIdType.MESH)

    loop(1, CHIPS, plane_peer)
    loop(1, Z * K, column_peer)


def met():
    pl.semaphore_wait(pltpu.get_barrier_semaphore(), CHIPS + Z * K - 2)


def loop(start, stop, body):
    def step(t, c):
        body(t)
        return c

    lax.fori_loop(start, stop, step, 0)


def split(x):
    hi = x.astype(BF16)
    return hi, (x - hi.astype(F32)).astype(BF16)


def dot(a, b):
    return lax.dot_general(a, b, (((1,), (0,)), ((), ())), preferred_element_type=F32)


def dot_t(a, b, precision=None):
    return lax.dot_general(a, b, (((1,), (1,)), ((), ())), preferred_element_type=F32, precision=precision)


def kernel(amp_hbm, fac, occ, out,
           amp, flip, slots, mine, sall, ball, s3, b3, y3, acc,
           sib, half, parts, at, gb, gb4, slot_a, slot_b, slot_b4, hd, hr, occs, gm, cm, hs, hout,
           in_sem, ex_send, ex_recv, a_send, a_recv, s_send, s_recv, w_send, w_recv, l_send, ring_send, ring_recv,
           q_send, q_recv, h_send, h_recv, c_send, c_recv, r_send, r_recv, f_send, f_recv, g_send, g_recv):
    p = lax.axis_index("pairs")
    w = lax.axis_index("aux")
    z, k = p // K, lax.rem(p, K)
    core = lax.rem(k, 2)
    m = w * K + k
    chip = w * 2 + k // 2
    other = p + 1 - 2 * core
    virt = amp.shape[1]
    cols = virt // W
    local = ball.shape[0]
    half_of = k // 2

    load = pltpu.make_async_copy(amp_hbm, amp, in_sem)
    load.start()
    greet(p, w, z, core, chip)
    met()

    def mine_of(gi, kk):
        return fac.at[pl.ds(kk * ball.shape[0] + GROUPS[gi][0], GROUPS[gi][1])]

    def my_rows(gi):
        return ball.at[pl.ds(*GROUPS[gi]), pl.ds(pl.multiple_of(8 * p, 8), 8), :]

    def region(gi, part, origin):
        row = origin * 32 + (half_of if part == 0 else 1 - half_of) * 16
        return ball.at[pl.ds(*GROUPS[gi]), pl.ds(pl.multiple_of(row, 16), 16), :]

    def keep(gi):
        return pltpu.make_async_copy(mine_of(gi, k), my_rows(gi), ex_recv.at[gi, 0])

    def exchange(gi, t):
        kk = lax.rem(half_of + t // 2, 2) * 2 + lax.rem(core + t, 2)
        return remote(mine_of(gi, kk), my_rows(gi), ex_send.at[gi, t], ex_recv.at[gi, t // 2], z * K + kk, w)

    def neighbour(way):
        return lax.rem(z + (1 if way == 0 else Z - 1), Z) * K

    def hops(way, gi, part):
        return 4 - (way + gi + part) % 2

    def launch(way, gi, t):
        kk = half_of * 2 + lax.rem(core + t, 2)
        return remote(mine_of(gi, kk), my_rows(gi), l_send.at[way, gi, t], ring_recv.at[way, gi, 0, 0],
                      neighbour(way) + kk, w)

    def ring(way, gi, part, h):
        here = region(gi, part, lax.rem(z + (Z - h if way == 0 else h), Z))
        return remote(here, here, ring_send.at[way, gi, part, h], ring_recv.at[way, gi, part, h],
                      neighbour(way) + k, w)

    def arrive(way, gi, part, h):
        here = region(gi, part, lax.rem(z + (Z - 1 - h if way == 0 else 1 + h), Z))
        remote(here, here, ring_send.at[way, gi, part, h], ring_recv.at[way, gi, part, h],
               neighbour(way) + k, w).wait_recv()

    def begin(gi):
        for way in range(2):
            for t in range(2):
                launch(way, gi, t).start()
        keep(gi).start()
        for t in range(1, K):
            exchange(gi, t).start()

    def begin_far(gi):
        wait_bytes(region(gi, 1, z), ex_recv.at[gi, 1])
        for way in range(2):
            ring(way, gi, 1, 0).start()

    def forward(gi, part, h):
        for way in range(2):
            if h < hops(way, gi, part):
                arrive(way, gi, part, h - 1)
                ring(way, gi, part, h).start()

    def landed(h):
        for gi in range(len(GROUPS)):
            for part in range(2):
                for way in range(2):
                    if hops(way, gi, part) == h + 1:
                        arrive(way, gi, part, h)

    for gi in range(len(GROUPS)):
        begin(gi)

    def straight(t):
        kk = lax.rem(k + t, K)
        src = amp.at[:, pl.ds(pl.multiple_of((w * K + kk) * 8, 8), 8), :]
        dst = slots.at[pl.ds(2 * k, 2)]
        if t == 0:
            return pltpu.make_async_copy(src, dst, a_recv)
        return remote(src, dst, a_send, a_recv, z * K + kk, w)

    def turned_far(s, kk):
        src = flip.at[s, pl.ds(pl.multiple_of((w * K + kk) * 8, 8), 8), :]
        return remote(src, slots.at[Z + z], a_send, a_recv, (2 * k + s) * K + kk, w)

    def turned_near(s, kk):
        src = flip.at[s, pl.ds(pl.multiple_of((w * K + kk) * 8, 8), 8), :]
        return pltpu.make_async_copy(src, slots.at[Z + z], a_recv)

    load.wait()
    for s in range(2):
        flip[s] = amp[s].T
    for s in range(2):
        for kk in range(K):
            here = jnp.logical_and(2 * k + s == z, kk == k)
            pl.when(here)(lambda s=s, kk=kk: turned_near(s, kk).start())
            pl.when(jnp.logical_not(here))(lambda s=s, kk=kk: turned_far(s, kk).start())
    for t in range(K):
        straight(t).start()
    for gi in range(len(GROUPS)):
        begin_far(gi)

    def share(t):
        n = lax.rem(chip + t, CHIPS)
        return remote(mine, sall.at[:, chip, core], s_send, s_recv, z * K + lax.rem(n, 2) * 2 + core, n // 2)

    wait_bytes(slots, a_recv)
    for d in range(OFFSETS):
        j = lax.rem(z + d, Z)
        mine[d] = slots[j] + slots[Z + j]
    pltpu.make_async_copy(mine, sall.at[:, chip, core], s_recv).start()
    loop(1, CHIPS, lambda t: share(t).start())
    for part in range(2):
        for gi in range(len(GROUPS)):
            forward(gi, part, 1)

    def occ_share(t):
        return remote(occ, occs.at[w], q_send, q_recv, p, lax.rem(w + t, W))

    pltpu.make_async_copy(occ, occs.at[w], q_recv).start()
    loop(1, W, lambda t: occ_share(t).start())
    at_w = pl.ds(pl.multiple_of(w * cols, cols), cols)
    for s in range(2):
        hd[:, s * cols:(s + 1) * cols] = flip[s, at_w, :].T
        hd[:, (2 + s) * cols:(3 + s) * cols] = amp[s, at_w, :].T
    for gi in range(len(GROUPS)):
        forward(gi, 0, 2)
    wait_bytes(sall.at[:, :, core], s_recv)
    across = remote(sall.at[:, :, core], sall.at[:, :, core], w_send, w_recv, other, w)
    across.start()
    for gi in range(len(GROUPS)):
        forward(gi, 1, 2)

    wait_bytes(occs, q_recv)
    g_sum = dot_t(occs[0], occs[0], highest)
    for n in range(1, W):
        g_sum = g_sum + dot_t(occs[n], occs[n], highest)
    gm[...] = g_sum
    by_k = [gm[pl.ds(kk, 8, stride=8), :] for kk in range(8)]
    for j in range(8):
        cm[pl.ds(j, 8, stride=8), :] = jnp.concatenate([x[:, j * 8:j * 8 + 8] for x in by_k], axis=1)

    wait_bytes(sall.at[:, :, 1 - core], w_recv)
    for d in range(OFFSETS):
        hi, lo = split(sall[d].reshape(virt, virt))
        s3[d, :virt], s3[d, virt:2 * virt], s3[d, 2 * virt:] = hi, lo, hi

    def first(origin):
        rows = pl.ds(pl.multiple_of(origin * 32, 32), 32)
        hi, lo = split(ball[:, rows, :])
        b3[:, rows, :virt], b3[:, rows, virt:2 * virt], b3[:, rows, 2 * virt:] = hi, hi, lo

        def one(d):
            y_hi, y_lo = split(dot(b3[:, rows, :].reshape(local * 32, 3 * virt), s3[d]))
            for q in range(local):
                at_q = q * 3 * virt
                y3[d, rows, at_q:at_q + virt] = y_hi[q * 32:(q + 1) * 32]
                y3[d, rows, at_q + virt:at_q + 2 * virt] = y_lo[q * 32:(q + 1) * 32]
                y3[d, rows, at_q + 2 * virt:at_q + 3 * virt] = y_hi[q * 32:(q + 1) * 32]

        loop(0, OFFSETS, one)

    def both(step):
        loop(0, 2, lambda t: first(lax.rem(z + step + t * (Z - 2 * step), Z)))

    def second(d):
        term = None
        for q in range(local):
            x = dot_t(y3[d, :, q * 3 * virt:(q + 1) * 3 * virt], b3[q])
            term = x if term is None else term + x
        acc[pl.ds(pl.multiple_of(d * virt, virt), virt)] = term

    sums = acc.reshape(OFFSETS, CHIPS, 2, 8, virt)

    def swap(d):
        return remote(sums.at[d, :, 1 - core], sib.at[d], c_send.at[d], c_recv.at[d], other, w)

    for gi in range(len(GROUPS)):
        wait_bytes(region(gi, 0, z), ex_recv.at[gi, 0])
    first(z)
    late = [(gi, part) for part in range(2) for gi in range(len(GROUPS))]
    share_of = len(late) // 4
    for gi, part in late[:share_of]:
        forward(gi, part, 3)
    both(1)
    for gi, part in late[share_of:2 * share_of]:
        forward(gi, part, 3)
    both(2)
    for gi, part in late[2 * share_of:]:
        forward(gi, part, 3)
    def hole_send(t):
        q = lax.rem(p + t, Z * K)
        return remote(hd.at[pl.ds(pl.multiple_of(q * 8, 8), 8), :], hr.at[p], h_send, h_recv, q, w)

    for gi in range(len(GROUPS)):
        for t in range(1, K):
            exchange(gi, t).wait_send()
        for way in range(2):
            for t in range(2):
                launch(way, gi, t).wait_send()
            for part in range(2):
                for h in range(1 - part, 3):
                    ring(way, gi, part, h).wait_send()
    for t in range(1, K):
        straight(t).wait_send()
    for s in range(2):
        for kk in range(K):
            here = jnp.logical_and(2 * k + s == z, kk == k)
            pl.when(jnp.logical_not(here))(lambda s=s, kk=kk: turned_far(s, kk).wait_send())
    across.wait_send()
    wait_bytes(parts.at[pl.ds(0, CHIPS - 1)], s_send)
    wait_bytes(occs.at[pl.ds(0, W - 1)], q_send)
    landed(2)
    both(3)
    landed(3)
    pltpu.make_async_copy(hd.at[pl.ds(pl.multiple_of(p * 8, 8), 8), :], hr.at[p], h_recv).start()
    loop(1, Z * K, lambda t: hole_send(t).start())
    first(lax.rem(z + 4, Z))


    def spread(t, e):
        n = lax.rem(chip + t, CHIPS)
        ds = pl.ds(SUMS[e][0], SUMS[e][1] - SUMS[e][0])
        return remote(half.at[ds, n], parts.at[chip, ds], r_send, r_recv.at[e], z * K + lax.rem(n, 2) * 2 + core, n // 2)

    def spread_group(e):
        low, high = SUMS[e]
        for d in range(low, high):
            swap(d).wait_recv()
            half[d] = sums[d, :, core] + sib[d]
        ds = pl.ds(low, high - low)
        pltpu.make_async_copy(half.at[ds, chip], parts.at[chip, ds], r_recv.at[e]).start()
        loop(1, CHIPS, lambda t: spread(t, e).start())

    def finish(d):
        second(d)
        swap(d).start()
        for e in range(len(SUMS) - 1):
            pl.when(d == SUMS[e][1])(lambda e=e: spread_group(e))

    loop(0, OFFSETS, finish)
    wait_bytes(hr, h_recv)
    flat = hr.reshape(Z * K * 8, 4 * cols)
    by_a = [flat[pl.ds(a, Z * K, stride=8), :] for a in range(8)]
    for s in range(2):
        for e in range(2):
            hs[e, pl.ds(s, Z * K, stride=2), :] = jnp.concatenate(
                [x[:, s * cols:(s + 1) * cols] for x in by_a[4 * e:4 * e + 4]], axis=1)
    for l2 in range(4):
        by_a = [flat[pl.ds(8 * l2 + a, 8, stride=32), :] for a in range(8)]
        for s in range(2):
            for e in range(2):
                at_row = 16 * l2 + 8 * s
                hs[e, at_row:at_row + 8, :] += jnp.concatenate(
                    [x[:, (2 + s) * cols:(3 + s) * cols] for x in by_a[4 * e:4 * e + 4]], axis=1)
    hole = [lax.dot_general(cm[...], hs[e], (((1,), (0,)), ((), ())), preferred_element_type=F32, precision=highest)
            for e in range(2)]
    for a in range(8):
        hout[pl.ds(a, 64, stride=8), :] = hole[a // 4][:, a % 4 * cols:(a % 4 + 1) * cols]

    spread_group(len(SUMS) - 1)

    for gi in range(len(GROUPS)):
        for way in range(2):
            for part in range(2):
                if hops(way, gi, part) == 4:
                    ring(way, gi, part, 3).wait_send()
    for d in range(OFFSETS):
        swap(d).wait_send()
    wait_bytes(parts.at[pl.ds(0, CHIPS - 1)], r_send)

    def gathered(e):
        low, high = SUMS[e]
        ds = pl.ds(low, high - low)
        wait_bytes(parts.at[:, ds], r_recv.at[e])
        total = parts[0, low:high]
        for n in range(1, CHIPS):
            total = total + parts[n, low:high]
        return [total[n] for n in range(high - low)]

    def col_send(t):
        q = lax.rem(p + t, Z * K)
        return remote(at.at[pl.ds(pl.multiple_of(q * 8, 8), 8), :], slot_a.at[p], f_send, f_recv, q, w)

    def row_send(e, ww):
        src, dst = ((gb, slot_b), (gb4, slot_b4))[e]
        return remote(src.at[ww], dst.at[z], g_send.at[e], g_recv.at[e], m, ww)

    def row_keep(e, ww):
        src, dst = ((gb, slot_b), (gb4, slot_b4))[e]
        return pltpu.make_async_copy(src.at[ww], dst.at[z], g_recv.at[e])

    def rows_start(e):
        for ww in range(W):
            here = jnp.logical_and(m == p, ww == w)
            pl.when(here)(lambda ww=ww: row_keep(e, ww).start())
            pl.when(jnp.logical_not(here))(lambda ww=ww: row_send(e, ww).start())

    def rows_sent(e):
        for ww in range(W):
            here = jnp.logical_and(m == p, ww == w)
            pl.when(jnp.logical_not(here))(lambda ww=ww: row_send(e, ww).wait_send())

    total = sum([gathered(e) for e in range(len(SUMS) - 1)], [])
    for ww in range(W):
        for d in range(1, 4):
            gb[ww, :, (d - 1) * cols:d * cols] = total[d][:, ww * cols:(ww + 1) * cols]
    at[...] = jnp.concatenate(total[:4], axis=0).T
    pltpu.make_async_copy(at.at[pl.ds(pl.multiple_of(p * 8, 8), 8), :], slot_a.at[p], f_recv).start()
    loop(1, Z * K, lambda t: col_send(t).start())
    rows_start(0)
    last, = gathered(len(SUMS) - 1)
    for ww in range(W):
        gb4[ww] = last[:, ww * cols:(ww + 1) * cols]
    rows_start(1)

    def result(pair, value):
        out[pair] = value + hout[pair * 8:pair * 8 + 8, :]

    wait_bytes(slot_a, f_recv)
    for zz in range(Z):
        tiles = [slot_a[zz * K + kk] for kk in range(K)]
        for d in range(4):
            result((zz + d) % 8 * 8 + zz, jnp.concatenate([tile[:, d * 8:d * 8 + 8] for tile in tiles], axis=1))
    wait_bytes(slot_b, g_recv.at[0])
    for zz in range(Z):
        tile = slot_b[zz]
        for d in range(1, 4):
            result(zz * 8 + (zz + d) % 8, tile[:, (d - 1) * cols:d * cols])
    wait_bytes(slot_a.at[pl.ds(0, Z * K - 1)], f_send)
    rows_sent(0)
    wait_bytes(slot_b4, g_recv.at[1])
    for zz in range(Z):
        result(zz * 8 + (zz + 4) % 8, slot_b4[zz])
    rows_sent(1)
    wait_bytes(hr.at[pl.ds(0, Z * K - 1)], h_send)


def shards(amplitudes, factors, occ_factors):
    aux_local, rows, virt = factors.shape
    occupied = occ_factors.shape[1]
    local = aux_local // K
    cols = virt // W
    occ = occ_factors.transpose(1, 2, 0).reshape(occupied * occupied, aux_local)
    vm = pl.BlockSpec(memory_space=pltpu.VMEM)
    anywhere = pl.BlockSpec(memory_space=pltpu.HBM)
    dma = pltpu.SemaphoreType.DMA
    v = pltpu.VMEM
    scratch = [
        v((2, virt, virt), F32), v((2, virt, virt), F32),
        v((2 * Z, 8, virt), F32), v((OFFSETS, 8, virt), F32),
        v((OFFSETS, CHIPS, 2, 8, virt), F32), v((local, virt, virt), F32),
        v((OFFSETS, 3 * virt, virt), BF16), v((local, virt, 3 * virt), BF16),
        v((OFFSETS, virt, local * 3 * virt), BF16),
        v((OFFSETS * virt, virt), F32),
        v((OFFSETS, CHIPS, 8, virt), F32), v((OFFSETS, CHIPS, 8, virt), F32),
        v((CHIPS, OFFSETS, 8, virt), F32),
        v((virt, 32), F32),
        v((W, 8, 3 * cols), F32), v((W, 8, cols), F32),
        v((Z * K, 8, 32), F32), v((Z, 8, 3 * cols), F32), v((Z, 8, cols), F32),
        v((virt, 128), F32), v((Z * K, 8, 128), F32),
        v((W, occupied * occupied, aux_local), F32),
        v((64, 64), F32), v((64, 64), F32), v((2, 64, 128), F32), v((64 * 8, cols), F32),
        dma(()), dma((len(GROUPS), K)), dma((len(GROUPS), 2)),
        dma(()), dma(()), dma(()), dma(()), dma(()), dma(()),
        dma((2, len(GROUPS), 2)), dma((2, len(GROUPS), 2, 4)), dma((2, len(GROUPS), 2, 4)),
        dma(()), dma(()), dma(()), dma(()), dma((OFFSETS,)), dma((OFFSETS,)), dma(()), dma((len(SUMS),)), dma(()), dma(()), dma((2,)), dma((2,)),
    ]
    return pl.pallas_call(
        kernel,
        out_shape=jax.ShapeDtypeStruct((occupied * occupied, rows, cols), F32),
        in_specs=[anywhere, anywhere, anywhere],
        out_specs=vm,
        scratch_shapes=scratch,
        compiler_params=pltpu.CompilerParams(
            collective_id=0, has_side_effects=True, vmem_limit_bytes=48 << 20),
        name="residual",
    )(pltpu.with_memory_space_constraint(amplitudes, pltpu.HBM), pltpu.with_memory_space_constraint(factors, pltpu.HBM),
      pltpu.with_memory_space_constraint(occ, pltpu.HBM))


def solution(mesh):
    placed = (P("pairs", None, None), P("aux", "pairs", None), P("aux", None, None))
    return jax.shard_map(
        shards, mesh=mesh, in_specs=placed, out_specs=P(None, "pairs", "aux"), check_vma=False
    )
```

```python
import jax
import jax.numpy as jnp
from jax import lax
from jax.experimental import pallas as pl
from jax.experimental.pallas import tpu as pltpu
from jax.sharding import PartitionSpec as P

highest = lax.Precision.HIGHEST
F32 = jnp.float32
BF16 = jnp.bfloat16

Z = 8
K = 4
W = 8
PLANE = K * W
CHIPS = PLANE // 2
OFFSETS = 5
GROUPS = ((0, 6), (6, 6))


SUMS = ((0, 2), (2, 4), (4, 5))


def remote(src, dst, send_sem, recv_sem, p, w):
    return pltpu.make_async_remote_copy(
        src_ref=src,
        dst_ref=dst,
        send_sem=send_sem,
        recv_sem=recv_sem,
        device_id={"pairs": p, "aux": w},
        device_id_type=pl.DeviceIdType.MESH,
    )


def wait_bytes(ref, sem):
    pltpu.make_async_copy(ref, ref, sem).wait()


def greet(p, w, z, core, chip):
    barrier = pltpu.get_barrier_semaphore()

    def plane_peer(t):
        n = lax.rem(chip + t, CHIPS)
        pl.semaphore_signal(
            barrier, inc=1, device_id={"pairs": z * K + lax.rem(n, 2) * 2 + core, "aux": n // 2},
            device_id_type=pl.DeviceIdType.MESH)

    def column_peer(t):
        pl.semaphore_signal(
            barrier, inc=1, device_id={"pairs": lax.rem(p + t, Z * K), "aux": w},
            device_id_type=pl.DeviceIdType.MESH)

    many(1, CHIPS, plane_peer)
    many(1, Z * K, column_peer)


def met():
    pl.semaphore_wait(pltpu.get_barrier_semaphore(), CHIPS + Z * K - 2)


def loop(start, stop, body):
    def step(t, c):
        body(t)
        return c

    lax.fori_loop(start, stop, step, 0)


def many(start, stop, body, wide=5):
    whole = (stop - start) // wide

    def step(n, c):
        for u in range(wide):
            body(start + n * wide + u)
        return c

    lax.fori_loop(0, whole, step, 0)
    for t in range(start + whole * wide, stop):
        body(t)


def split(x):
    hi = x.astype(BF16)
    return hi, (x - hi.astype(F32)).astype(BF16)


def dot(a, b):
    return lax.dot_general(a, b, (((1,), (0,)), ((), ())), preferred_element_type=F32)


def dot_t(a, b, precision=None):
    return lax.dot_general(a, b, (((1,), (1,)), ((), ())), preferred_element_type=F32, precision=precision)


def kernel(amp_hbm, fac, occ, out,
           amp, flip, slots, mine, sall, ball, s3, b3, y3, acc,
           sib, half, parts, at, gb, gb4, slot_a, slot_b, slot_b4, hd, hr, occs, gm, cm, hs, hout,
           in_sem, ex_send, ex_recv, a_send, a_recv, s_send, s_recv, w_send, w_recv, l_send, ring_send, ring_recv,
           q_send, q_recv, h_send, h_recv, c_send, c_recv, r_send, r_recv, f_send, f_recv, g_send, g_recv):
    p = lax.axis_index("pairs")
    w = lax.axis_index("aux")
    z, k = p // K, lax.rem(p, K)
    core = lax.rem(k, 2)
    m = w * K + k
    chip = w * 2 + k // 2
    other = p + 1 - 2 * core
    virt = amp.shape[1]
    cols = virt // W
    local = ball.shape[0]
    half_of = k // 2

    load = pltpu.make_async_copy(amp_hbm, amp, in_sem)
    load.start()
    greet(p, w, z, core, chip)
    met()

    def mine_of(gi, kk):
        return fac.at[pl.ds(kk * ball.shape[0] + GROUPS[gi][0], GROUPS[gi][1])]

    def my_rows(gi):
        return ball.at[pl.ds(*GROUPS[gi]), pl.ds(pl.multiple_of(8 * p, 8), 8), :]

    def region(gi, part, origin):
        row = origin * 32 + (half_of if part == 0 else 1 - half_of) * 16
        return ball.at[pl.ds(*GROUPS[gi]), pl.ds(pl.multiple_of(row, 16), 16), :]

    def keep(gi):
        return pltpu.make_async_copy(mine_of(gi, k), my_rows(gi), ex_recv.at[gi, 0])

    def exchange(gi, t):
        kk = lax.rem(half_of + t // 2, 2) * 2 + lax.rem(core + t, 2)
        return remote(mine_of(gi, kk), my_rows(gi), ex_send.at[gi, t], ex_recv.at[gi, t // 2], z * K + kk, w)

    def neighbour(way):
        return lax.rem(z + (1 if way == 0 else Z - 1), Z) * K

    def hops(way, gi, part):
        return 4 - (way + gi + part) % 2

    def launch(way, gi, t):
        kk = half_of * 2 + lax.rem(core + t, 2)
        return remote(mine_of(gi, kk), my_rows(gi), l_send.at[way, gi, t], ring_recv.at[way, gi, 0, 0],
                      neighbour(way) + kk, w)

    def ring(way, gi, part, h):
        here = region(gi, part, lax.rem(z + (Z - h if way == 0 else h), Z))
        return remote(here, here, ring_send.at[way, gi, part, h], ring_recv.at[way, gi, part, h],
                      neighbour(way) + k, w)

    def arrive(way, gi, part, h):
        here = region(gi, part, lax.rem(z + (Z - 1 - h if way == 0 else 1 + h), Z))
        remote(here, here, ring_send.at[way, gi, part, h], ring_recv.at[way, gi, part, h],
               neighbour(way) + k, w).wait_recv()

    def begin(gi):
        for way in range(2):
            for t in range(2):
                launch(way, gi, t).start()
        keep(gi).start()
        for t in range(1, K):
            exchange(gi, t).start()

    def begin_far(gi):
        wait_bytes(region(gi, 1, z), ex_recv.at[gi, 1])
        for way in range(2):
            ring(way, gi, 1, 0).start()

    def forward(gi, part, h):
        for way in range(2):
            if h < hops(way, gi, part):
                arrive(way, gi, part, h - 1)
                ring(way, gi, part, h).start()

    def landed(h):
        for gi in range(len(GROUPS)):
            for part in range(2):
                for way in range(2):
                    if hops(way, gi, part) == h + 1:
                        arrive(way, gi, part, h)

    for gi in range(len(GROUPS)):
        begin(gi)

    def straight(t):
        kk = lax.rem(k + t, K)
        src = amp.at[:, pl.ds(pl.multiple_of((w * K + kk) * 8, 8), 8), :]
        dst = slots.at[pl.ds(2 * k, 2)]
        if t == 0:
            return pltpu.make_async_copy(src, dst, a_recv)
        return remote(src, dst, a_send, a_recv, z * K + kk, w)

    def turned_far(s, kk):
        src = flip.at[s, pl.ds(pl.multiple_of((w * K + kk) * 8, 8), 8), :]
        return remote(src, slots.at[Z + z], a_send, a_recv, (2 * k + s) * K + kk, w)

    def turned_near(s, kk):
        src = flip.at[s, pl.ds(pl.multiple_of((w * K + kk) * 8, 8), 8), :]
        return pltpu.make_async_copy(src, slots.at[Z + z], a_recv)

    load.wait()
    for s in range(2):
        flip[s] = amp[s].T
    for s in range(2):
        for kk in range(K):
            here = jnp.logical_and(2 * k + s == z, kk == k)
            pl.when(here)(lambda s=s, kk=kk: turned_near(s, kk).start())
            pl.when(jnp.logical_not(here))(lambda s=s, kk=kk: turned_far(s, kk).start())
    for t in range(K):
        straight(t).start()
    for gi in range(len(GROUPS)):
        begin_far(gi)

    def share(t):
        n = lax.rem(chip + t, CHIPS)
        return remote(mine, sall.at[:, chip, core], s_send, s_recv, z * K + lax.rem(n, 2) * 2 + core, n // 2)

    wait_bytes(slots, a_recv)
    for d in range(OFFSETS):
        j = lax.rem(z + d, Z)
        mine[d] = slots[j] + slots[Z + j]
    pltpu.make_async_copy(mine, sall.at[:, chip, core], s_recv).start()
    many(1, CHIPS, lambda t: share(t).start())
    for part in range(2):
        for gi in range(len(GROUPS)):
            forward(gi, part, 1)

    def occ_share(t):
        return remote(occ, occs.at[w], q_send, q_recv, p, lax.rem(w + t, W))

    pltpu.make_async_copy(occ, occs.at[w], q_recv).start()
    many(1, W, lambda t: occ_share(t).start())
    at_w = pl.ds(pl.multiple_of(w * cols, cols), cols)
    for s in range(2):
        hd[:, s * cols:(s + 1) * cols] = flip[s, at_w, :].T
        hd[:, (2 + s) * cols:(3 + s) * cols] = amp[s, at_w, :].T
    for gi in range(len(GROUPS)):
        forward(gi, 0, 2)
    wait_bytes(sall.at[:, :, core], s_recv)
    across = remote(sall.at[:, :, core], sall.at[:, :, core], w_send, w_recv, other, w)
    across.start()
    for gi in range(len(GROUPS)):
        forward(gi, 1, 2)

    wait_bytes(occs, q_recv)
    g_sum = dot_t(occs[0], occs[0], highest)
    for n in range(1, W):
        g_sum = g_sum + dot_t(occs[n], occs[n], highest)
    gm[...] = g_sum
    by_k = [gm[pl.ds(kk, 8, stride=8), :] for kk in range(8)]
    for j in range(8):
        cm[pl.ds(j, 8, stride=8), :] = jnp.concatenate([x[:, j * 8:j * 8 + 8] for x in by_k], axis=1)

    wait_bytes(sall.at[:, :, 1 - core], w_recv)
    for d in range(OFFSETS):
        hi, lo = split(sall[d].reshape(virt, virt))
        s3[d, :virt], s3[d, virt:2 * virt], s3[d, 2 * virt:] = hi, lo, hi

    def first(origin):
        rows = pl.ds(pl.multiple_of(origin * 32, 32), 32)
        hi, lo = split(ball[:, rows, :])
        b3[:, rows, :virt], b3[:, rows, virt:2 * virt], b3[:, rows, 2 * virt:] = hi, hi, lo

        def one(d):
            y_hi, y_lo = split(dot(b3[:, rows, :].reshape(local * 32, 3 * virt), s3[d]))
            for q in range(local):
                at_q = q * 3 * virt
                y3[d, rows, at_q:at_q + virt] = y_hi[q * 32:(q + 1) * 32]
                y3[d, rows, at_q + virt:at_q + 2 * virt] = y_lo[q * 32:(q + 1) * 32]
                y3[d, rows, at_q + 2 * virt:at_q + 3 * virt] = y_hi[q * 32:(q + 1) * 32]

        loop(0, OFFSETS, one)

    def both(step):
        loop(0, 2, lambda t: first(lax.rem(z + step + t * (Z - 2 * step), Z)))

    def second(d):
        term = None
        for q in range(local):
            x = dot_t(y3[d, :, q * 3 * virt:(q + 1) * 3 * virt], b3[q])
            term = x if term is None else term + x
        acc[pl.ds(pl.multiple_of(d * virt, virt), virt)] = term

    sums = acc.reshape(OFFSETS, CHIPS, 2, 8, virt)

    def swap(d):
        return remote(sums.at[d, :, 1 - core], sib.at[d], c_send.at[d], c_recv.at[d], other, w)

    for gi in range(len(GROUPS)):
        wait_bytes(region(gi, 0, z), ex_recv.at[gi, 0])
    first(z)
    late = [(gi, part) for part in range(2) for gi in range(len(GROUPS))]
    share_of = len(late) // 4
    for gi, part in late[:share_of]:
        forward(gi, part, 3)
    both(1)
    for gi, part in late[share_of:2 * share_of]:
        forward(gi, part, 3)
    both(2)
    for gi, part in late[2 * share_of:]:
        forward(gi, part, 3)
    def hole_send(t):
        q = lax.rem(p + t, Z * K)
        return remote(hd.at[pl.ds(pl.multiple_of(q * 8, 8), 8), :], hr.at[p], h_send, h_recv, q, w)

    for gi in range(len(GROUPS)):
        for t in range(1, K):
            exchange(gi, t).wait_send()
        for way in range(2):
            for t in range(2):
                launch(way, gi, t).wait_send()
            for part in range(2):
                for h in range(1 - part, 3):
                    ring(way, gi, part, h).wait_send()
    for t in range(1, K):
        straight(t).wait_send()
    for s in range(2):
        for kk in range(K):
            here = jnp.logical_and(2 * k + s == z, kk == k)
            pl.when(jnp.logical_not(here))(lambda s=s, kk=kk: turned_far(s, kk).wait_send())
    across.wait_send()
    wait_bytes(parts.at[pl.ds(0, CHIPS - 1)], s_send)
    wait_bytes(occs.at[pl.ds(0, W - 1)], q_send)
    landed(2)
    both(3)
    landed(3)
    pltpu.make_async_copy(hd.at[pl.ds(pl.multiple_of(p * 8, 8), 8), :], hr.at[p], h_recv).start()
    many(1, Z * K, lambda t: hole_send(t).start())
    first(lax.rem(z + 4, Z))


    def spread(t, e):
        n = lax.rem(chip + t, CHIPS)
        ds = pl.ds(SUMS[e][0], SUMS[e][1] - SUMS[e][0])
        return remote(half.at[ds, n], parts.at[chip, ds], r_send, r_recv.at[e], z * K + lax.rem(n, 2) * 2 + core, n // 2)

    def spread_group(e):
        low, high = SUMS[e]
        for d in range(low, high):
            swap(d).wait_recv()
            half[d] = sums[d, :, core] + sib[d]
        ds = pl.ds(low, high - low)
        pltpu.make_async_copy(half.at[ds, chip], parts.at[chip, ds], r_recv.at[e]).start()
        many(1, CHIPS, lambda t: spread(t, e).start())

    def finish(d):
        second(d)
        swap(d).start()
        for e in range(len(SUMS) - 1):
            pl.when(d == SUMS[e][1])(lambda e=e: spread_group(e))

    loop(0, OFFSETS, finish)
    wait_bytes(hr, h_recv)
    flat = hr.reshape(Z * K * 8, 4 * cols)
    by_a = [flat[pl.ds(a, Z * K, stride=8), :] for a in range(8)]
    for s in range(2):
        for e in range(2):
            hs[e, pl.ds(s, Z * K, stride=2), :] = jnp.concatenate(
                [x[:, s * cols:(s + 1) * cols] for x in by_a[4 * e:4 * e + 4]], axis=1)
    for l2 in range(4):
        by_a = [flat[pl.ds(8 * l2 + a, 8, stride=32), :] for a in range(8)]
        for s in range(2):
            for e in range(2):
                at_row = 16 * l2 + 8 * s
                hs[e, at_row:at_row + 8, :] += jnp.concatenate(
                    [x[:, (2 + s) * cols:(3 + s) * cols] for x in by_a[4 * e:4 * e + 4]], axis=1)
    hole = [lax.dot_general(cm[...], hs[e], (((1,), (0,)), ((), ())), preferred_element_type=F32, precision=highest)
            for e in range(2)]
    for a in range(8):
        hout[pl.ds(a, 64, stride=8), :] = hole[a // 4][:, a % 4 * cols:(a % 4 + 1) * cols]

    spread_group(len(SUMS) - 1)

    for gi in range(len(GROUPS)):
        for way in range(2):
            for part in range(2):
                if hops(way, gi, part) == 4:
                    ring(way, gi, part, 3).wait_send()
    for d in range(OFFSETS):
        swap(d).wait_send()
    wait_bytes(parts.at[pl.ds(0, CHIPS - 1)], r_send)

    def gathered(e):
        low, high = SUMS[e]
        ds = pl.ds(low, high - low)
        wait_bytes(parts.at[:, ds], r_recv.at[e])
        total = parts[0, low:high]
        for n in range(1, CHIPS):
            total = total + parts[n, low:high]
        return [total[n] for n in range(high - low)]

    def col_send(t):
        q = lax.rem(p + t, Z * K)
        return remote(at.at[pl.ds(pl.multiple_of(q * 8, 8), 8), :], slot_a.at[p], f_send, f_recv, q, w)

    def row_send(e, ww):
        src, dst = ((gb, slot_b), (gb4, slot_b4))[e]
        return remote(src.at[ww], dst.at[z], g_send.at[e], g_recv.at[e], m, ww)

    def row_keep(e, ww):
        src, dst = ((gb, slot_b), (gb4, slot_b4))[e]
        return pltpu.make_async_copy(src.at[ww], dst.at[z], g_recv.at[e])

    def rows_start(e):
        for ww in range(W):
            here = jnp.logical_and(m == p, ww == w)
            pl.when(here)(lambda ww=ww: row_keep(e, ww).start())
            pl.when(jnp.logical_not(here))(lambda ww=ww: row_send(e, ww).start())

    def rows_sent(e):
        for ww in range(W):
            here = jnp.logical_and(m == p, ww == w)
            pl.when(jnp.logical_not(here))(lambda ww=ww: row_send(e, ww).wait_send())

    total = sum([gathered(e) for e in range(len(SUMS) - 1)], [])
    for ww in range(W):
        for d in range(1, 4):
            gb[ww, :, (d - 1) * cols:d * cols] = total[d][:, ww * cols:(ww + 1) * cols]
    at[...] = jnp.concatenate(total[:4], axis=0).T
    pltpu.make_async_copy(at.at[pl.ds(pl.multiple_of(p * 8, 8), 8), :], slot_a.at[p], f_recv).start()
    many(1, Z * K, lambda t: col_send(t).start())
    rows_start(0)
    last, = gathered(len(SUMS) - 1)
    for ww in range(W):
        gb4[ww] = last[:, ww * cols:(ww + 1) * cols]
    rows_start(1)

    def result(pair, value):
        out[pair] = value + hout[pair * 8:pair * 8 + 8, :]

    wait_bytes(slot_a, f_recv)
    for zz in range(Z):
        tiles = [slot_a[zz * K + kk] for kk in range(K)]
        for d in range(4):
            result((zz + d) % 8 * 8 + zz, jnp.concatenate([tile[:, d * 8:d * 8 + 8] for tile in tiles], axis=1))
    wait_bytes(slot_b, g_recv.at[0])
    for zz in range(Z):
        tile = slot_b[zz]
        for d in range(1, 4):
            result(zz * 8 + (zz + d) % 8, tile[:, (d - 1) * cols:d * cols])
    wait_bytes(slot_a.at[pl.ds(0, Z * K - 1)], f_send)
    rows_sent(0)
    wait_bytes(slot_b4, g_recv.at[1])
    for zz in range(Z):
        result(zz * 8 + (zz + 4) % 8, slot_b4[zz])
    rows_sent(1)
    wait_bytes(hr.at[pl.ds(0, Z * K - 1)], h_send)


def shards(amplitudes, factors, occ_factors):
    aux_local, rows, virt = factors.shape
    occupied = occ_factors.shape[1]
    local = aux_local // K
    cols = virt // W
    occ = occ_factors.transpose(1, 2, 0).reshape(occupied * occupied, aux_local)
    vm = pl.BlockSpec(memory_space=pltpu.VMEM)
    anywhere = pl.BlockSpec(memory_space=pltpu.HBM)
    dma = pltpu.SemaphoreType.DMA
    v = pltpu.VMEM
    scratch = [
        v((2, virt, virt), F32), v((2, virt, virt), F32),
        v((2 * Z, 8, virt), F32), v((OFFSETS, 8, virt), F32),
        v((OFFSETS, CHIPS, 2, 8, virt), F32), v((local, virt, virt), F32),
        v((OFFSETS, 3 * virt, virt), BF16), v((local, virt, 3 * virt), BF16),
        v((OFFSETS, virt, local * 3 * virt), BF16),
        v((OFFSETS * virt, virt), F32),
        v((OFFSETS, CHIPS, 8, virt), F32), v((OFFSETS, CHIPS, 8, virt), F32),
        v((CHIPS, OFFSETS, 8, virt), F32),
        v((virt, 32), F32),
        v((W, 8, 3 * cols), F32), v((W, 8, cols), F32),
        v((Z * K, 8, 32), F32), v((Z, 8, 3 * cols), F32), v((Z, 8, cols), F32),
        v((virt, 128), F32), v((Z * K, 8, 128), F32),
        v((W, occupied * occupied, aux_local), F32),
        v((64, 64), F32), v((64, 64), F32), v((2, 64, 128), F32), v((64 * 8, cols), F32),
        dma(()), dma((len(GROUPS), K)), dma((len(GROUPS), 2)),
        dma(()), dma(()), dma(()), dma(()), dma(()), dma(()),
        dma((2, len(GROUPS), 2)), dma((2, len(GROUPS), 2, 4)), dma((2, len(GROUPS), 2, 4)),
        dma(()), dma(()), dma(()), dma(()), dma((OFFSETS,)), dma((OFFSETS,)), dma(()), dma((len(SUMS),)), dma(()), dma(()), dma((2,)), dma((2,)),
    ]
    return pl.pallas_call(
        kernel,
        out_shape=jax.ShapeDtypeStruct((occupied * occupied, rows, cols), F32),
        in_specs=[anywhere, anywhere, anywhere],
        out_specs=vm,
        scratch_shapes=scratch,
        compiler_params=pltpu.CompilerParams(
            collective_id=0, has_side_effects=True, vmem_limit_bytes=48 << 20),
        name="residual",
    )(pltpu.with_memory_space_constraint(amplitudes, pltpu.HBM), pltpu.with_memory_space_constraint(factors, pltpu.HBM),
      pltpu.with_memory_space_constraint(occ, pltpu.HBM))


def solution(mesh):
    placed = (P("pairs", None, None), P("aux", "pairs", None), P("aux", None, None))
    return jax.shard_map(
        shards, mesh=mesh, in_specs=placed, out_specs=P(None, "pairs", "aux"), check_vma=False
    )
```

```python
import jax
import jax.numpy as jnp
from jax import lax
from jax.experimental import pallas as pl
from jax.experimental.pallas import tpu as pltpu
from jax.sharding import PartitionSpec as P

highest = lax.Precision.HIGHEST
F32 = jnp.float32
BF16 = jnp.bfloat16

Z = 8
K = 4
W = 8
PLANE = K * W
CHIPS = PLANE // 2
OFFSETS = 5
GROUPS = ((0, 6), (6, 6))


SUMS = ((0, 2), (2, 4), (4, 5))


def remote(src, dst, send_sem, recv_sem, p, w):
    return pltpu.make_async_remote_copy(
        src_ref=src,
        dst_ref=dst,
        send_sem=send_sem,
        recv_sem=recv_sem,
        device_id={"pairs": p, "aux": w},
        device_id_type=pl.DeviceIdType.MESH,
    )


def wait_bytes(ref, sem):
    pltpu.make_async_copy(ref, ref, sem).wait()


def greet(p, w, z, core, chip):
    barrier = pltpu.get_barrier_semaphore()

    def plane_peer(t):
        n = lax.rem(chip + t, CHIPS)
        pl.semaphore_signal(
            barrier, inc=1, device_id={"pairs": z * K + lax.rem(n, 2) * 2 + core, "aux": n // 2},
            device_id_type=pl.DeviceIdType.MESH)

    def column_peer(t):
        pl.semaphore_signal(
            barrier, inc=1, device_id={"pairs": lax.rem(p + t, Z * K), "aux": w},
            device_id_type=pl.DeviceIdType.MESH)

    many(1, CHIPS, plane_peer)
    many(1, Z * K, column_peer)


def met():
    pl.semaphore_wait(pltpu.get_barrier_semaphore(), CHIPS + Z * K - 2)


def loop(start, stop, body):
    def step(t, c):
        body(t)
        return c

    lax.fori_loop(start, stop, step, 0)


def many(start, stop, body, wide=5):
    whole = (stop - start) // wide

    def step(n, c):
        for u in range(wide):
            body(start + n * wide + u)
        return c

    lax.fori_loop(0, whole, step, 0)
    for t in range(start + whole * wide, stop):
        body(t)


def split(x):
    hi = x.astype(BF16)
    return hi, (x - hi.astype(F32)).astype(BF16)


def dot(a, b):
    return lax.dot_general(a, b, (((1,), (0,)), ((), ())), preferred_element_type=F32)


def dot_t(a, b, precision=None):
    return lax.dot_general(a, b, (((1,), (1,)), ((), ())), preferred_element_type=F32, precision=precision)


def kernel(amp_hbm, fac, occ, out,
           amp, flip, slots, mine, sall, ball, s3, b3, y3, acc,
           sib, half, parts, at, gb, gb4, slot_a, slot_b, slot_b4, hd, hr, occs, gm, cm, hs, hout,
           in_sem, ex_send, ex_recv, a_send, a_recv, s_send, s_recv, w_send, w_recv, l_send, ring_send, ring_recv,
           q_send, q_recv, h_send, h_recv, c_send, c_recv, r_send, r_recv, f_send, f_recv, g_send, g_recv):
    p = lax.axis_index("pairs")
    w = lax.axis_index("aux")
    z, k = p // K, lax.rem(p, K)
    core = lax.rem(k, 2)
    m = w * K + k
    chip = w * 2 + k // 2
    other = p + 1 - 2 * core
    virt = amp.shape[1]
    cols = virt // W
    local = ball.shape[0]
    half_of = k // 2

    load = pltpu.make_async_copy(amp_hbm, amp, in_sem)
    load.start()
    greet(p, w, z, core, chip)
    met()

    def mine_of(gi, kk):
        return fac.at[pl.ds(kk * ball.shape[0] + GROUPS[gi][0], GROUPS[gi][1])]

    def my_rows(gi):
        return ball.at[pl.ds(*GROUPS[gi]), pl.ds(pl.multiple_of(8 * p, 8), 8), :]

    def region(gi, part, origin):
        row = origin * 32 + (half_of if part == 0 else 1 - half_of) * 16
        return ball.at[pl.ds(*GROUPS[gi]), pl.ds(pl.multiple_of(row, 16), 16), :]

    def keep(gi):
        return pltpu.make_async_copy(mine_of(gi, k), my_rows(gi), ex_recv.at[gi, 0])

    def exchange(gi, t):
        kk = lax.rem(half_of + t // 2, 2) * 2 + lax.rem(core + t, 2)
        return remote(mine_of(gi, kk), my_rows(gi), ex_send.at[gi, t], ex_recv.at[gi, t // 2], z * K + kk, w)

    def neighbour(way):
        return lax.rem(z + (1 if way == 0 else Z - 1), Z) * K

    def hops(way, gi, part):
        return 4 - (way + gi + part) % 2

    def launch(way, gi, t):
        kk = half_of * 2 + lax.rem(core + t, 2)
        return remote(mine_of(gi, kk), my_rows(gi), l_send.at[way, gi, t], ring_recv.at[way, gi, 0, 0],
                      neighbour(way) + kk, w)

    def ring(way, gi, part, h):
        here = region(gi, part, lax.rem(z + (Z - h if way == 0 else h), Z))
        return remote(here, here, ring_send.at[way, gi, part, h], ring_recv.at[way, gi, part, h],
                      neighbour(way) + k, w)

    def arrive(way, gi, part, h):
        here = region(gi, part, lax.rem(z + (Z - 1 - h if way == 0 else 1 + h), Z))
        remote(here, here, ring_send.at[way, gi, part, h], ring_recv.at[way, gi, part, h],
               neighbour(way) + k, w).wait_recv()

    def begin(gi):
        for way in range(2):
            for t in range(2):
                launch(way, gi, t).start()
        keep(gi).start()
        for t in range(1, K):
            exchange(gi, t).start()

    def begin_far(gi):
        wait_bytes(region(gi, 1, z), ex_recv.at[gi, 1])
        for way in range(2):
            ring(way, gi, 1, 0).start()

    def forward(gi, part, h):
        for way in range(2):
            if h < hops(way, gi, part):
                arrive(way, gi, part, h - 1)
                ring(way, gi, part, h).start()

    def landed(h):
        for gi in range(len(GROUPS)):
            for part in range(2):
                for way in range(2):
                    if hops(way, gi, part) == h + 1:
                        arrive(way, gi, part, h)

    for gi in range(len(GROUPS)):
        begin(gi)

    def straight(t):
        kk = lax.rem(k + t, K)
        src = amp.at[:, pl.ds(pl.multiple_of((w * K + kk) * 8, 8), 8), :]
        dst = slots.at[pl.ds(2 * k, 2)]
        if t == 0:
            return pltpu.make_async_copy(src, dst, a_recv)
        return remote(src, dst, a_send, a_recv, z * K + kk, w)

    def turned_far(s, kk):
        src = flip.at[s, pl.ds(pl.multiple_of((w * K + kk) * 8, 8), 8), :]
        return remote(src, slots.at[Z + z], a_send, a_recv, (2 * k + s) * K + kk, w)

    def turned_near(s, kk):
        src = flip.at[s, pl.ds(pl.multiple_of((w * K + kk) * 8, 8), 8), :]
        return pltpu.make_async_copy(src, slots.at[Z + z], a_recv)

    load.wait()
    for s in range(2):
        flip[s] = amp[s].T
    for s in range(2):
        for kk in range(K):
            here = jnp.logical_and(2 * k + s == z, kk == k)
            pl.when(here)(lambda s=s, kk=kk: turned_near(s, kk).start())
            pl.when(jnp.logical_not(here))(lambda s=s, kk=kk: turned_far(s, kk).start())
    for t in range(K):
        straight(t).start()
    for gi in range(len(GROUPS)):
        begin_far(gi)

    def share(t):
        n = lax.rem(chip + t, CHIPS)
        return remote(mine, sall.at[:, chip, core], s_send, s_recv, z * K + lax.rem(n, 2) * 2 + core, n // 2)

    wait_bytes(slots, a_recv)
    for d in range(OFFSETS):
        j = lax.rem(z + d, Z)
        mine[d] = slots[j] + slots[Z + j]
    pltpu.make_async_copy(mine, sall.at[:, chip, core], s_recv).start()
    many(1, CHIPS, lambda t: share(t).start())
    for part in range(2):
        for gi in range(len(GROUPS)):
            forward(gi, part, 1)

    def occ_share(t):
        return remote(occ, occs.at[w], q_send, q_recv, p, lax.rem(w + t, W))

    pltpu.make_async_copy(occ, occs.at[w], q_recv).start()
    many(1, W, lambda t: occ_share(t).start())
    at_w = pl.ds(pl.multiple_of(w * cols, cols), cols)
    for s in range(2):
        hd[:, s * cols:(s + 1) * cols] = flip[s, at_w, :].T
        hd[:, (2 + s) * cols:(3 + s) * cols] = amp[s, at_w, :].T
    for gi in range(len(GROUPS)):
        forward(gi, 0, 2)
    wait_bytes(sall.at[:, :, core], s_recv)
    across = remote(sall.at[:, :, core], sall.at[:, :, core], w_send, w_recv, other, w)
    across.start()
    for gi in range(len(GROUPS)):
        forward(gi, 1, 2)

    wait_bytes(occs, q_recv)
    g_sum = dot_t(occs[0], occs[0], highest)
    for n in range(1, W):
        g_sum = g_sum + dot_t(occs[n], occs[n], highest)
    gm[...] = g_sum
    by_k = [gm[pl.ds(kk, 8, stride=8), :] for kk in range(8)]
    for j in range(8):
        cm[pl.ds(j, 8, stride=8), :] = jnp.concatenate([x[:, j * 8:j * 8 + 8] for x in by_k], axis=1)

    wait_bytes(sall.at[:, :, 1 - core], w_recv)
    for d in range(OFFSETS):
        hi, lo = split(sall[d].reshape(virt, virt))
        s3[d, :virt], s3[d, virt:2 * virt], s3[d, 2 * virt:] = hi, lo, hi

    def first(origin):
        rows = pl.ds(pl.multiple_of(origin * 32, 32), 32)
        hi, lo = split(ball[:, rows, :])
        b3[:, rows, :virt], b3[:, rows, virt:2 * virt], b3[:, rows, 2 * virt:] = hi, hi, lo

        def one(d):
            y_hi, y_lo = split(dot(b3[:, rows, :].reshape(local * 32, 3 * virt), s3[d]))
            for q in range(local):
                at_q = q * 3 * virt
                y3[d, rows, at_q:at_q + virt] = y_hi[q * 32:(q + 1) * 32]
                y3[d, rows, at_q + virt:at_q + 2 * virt] = y_lo[q * 32:(q + 1) * 32]
                y3[d, rows, at_q + 2 * virt:at_q + 3 * virt] = y_hi[q * 32:(q + 1) * 32]

        for d in range(OFFSETS):
            one(d)

    def both(step):
        loop(0, 2, lambda t: first(lax.rem(z + step + t * (Z - 2 * step), Z)))

    def second(d):
        term = None
        for q in range(local):
            x = dot_t(y3[d, :, q * 3 * virt:(q + 1) * 3 * virt], b3[q])
            term = x if term is None else term + x
        acc[pl.ds(pl.multiple_of(d * virt, virt), virt)] = term

    sums = acc.reshape(OFFSETS, CHIPS, 2, 8, virt)

    def swap(d):
        return remote(sums.at[d, :, 1 - core], sib.at[d], c_send.at[d], c_recv.at[d], other, w)

    for gi in range(len(GROUPS)):
        wait_bytes(region(gi, 0, z), ex_recv.at[gi, 0])
    first(z)
    late = [(gi, part) for part in range(2) for gi in range(len(GROUPS))]
    share_of = len(late) // 4
    for gi, part in late[:share_of]:
        forward(gi, part, 3)
    both(1)
    for gi, part in late[share_of:2 * share_of]:
        forward(gi, part, 3)
    both(2)
    for gi, part in late[2 * share_of:]:
        forward(gi, part, 3)
    def hole_send(t):
        q = lax.rem(p + t, Z * K)
        return remote(hd.at[pl.ds(pl.multiple_of(q * 8, 8), 8), :], hr.at[p], h_send, h_recv, q, w)

    for gi in range(len(GROUPS)):
        for t in range(1, K):
            exchange(gi, t).wait_send()
        for way in range(2):
            for t in range(2):
                launch(way, gi, t).wait_send()
            for part in range(2):
                for h in range(1 - part, 3):
                    ring(way, gi, part, h).wait_send()
    for t in range(1, K):
        straight(t).wait_send()
    for s in range(2):
        for kk in range(K):
            here = jnp.logical_and(2 * k + s == z, kk == k)
            pl.when(jnp.logical_not(here))(lambda s=s, kk=kk: turned_far(s, kk).wait_send())
    across.wait_send()
    wait_bytes(parts.at[pl.ds(0, CHIPS - 1)], s_send)
    wait_bytes(occs.at[pl.ds(0, W - 1)], q_send)
    landed(2)
    both(3)
    landed(3)
    pltpu.make_async_copy(hd.at[pl.ds(pl.multiple_of(p * 8, 8), 8), :], hr.at[p], h_recv).start()
    many(1, Z * K, lambda t: hole_send(t).start())
    first(lax.rem(z + 4, Z))


    def spread(t, e):
        n = lax.rem(chip + t, CHIPS)
        ds = pl.ds(SUMS[e][0], SUMS[e][1] - SUMS[e][0])
        return remote(half.at[ds, n], parts.at[chip, ds], r_send, r_recv.at[e], z * K + lax.rem(n, 2) * 2 + core, n // 2)

    def spread_group(e):
        low, high = SUMS[e]
        for d in range(low, high):
            swap(d).wait_recv()
            half[d] = sums[d, :, core] + sib[d]
        ds = pl.ds(low, high - low)
        pltpu.make_async_copy(half.at[ds, chip], parts.at[chip, ds], r_recv.at[e]).start()
        many(1, CHIPS, lambda t: spread(t, e).start())

    def finish(d):
        second(d)
        swap(d).start()
        for e in range(len(SUMS) - 1):
            pl.when(d == SUMS[e][1])(lambda e=e: spread_group(e))

    loop(0, OFFSETS, finish)
    wait_bytes(hr, h_recv)
    flat = hr.reshape(Z * K * 8, 4 * cols)
    by_a = [flat[pl.ds(a, Z * K, stride=8), :] for a in range(8)]
    for s in range(2):
        for e in range(2):
            hs[e, pl.ds(s, Z * K, stride=2), :] = jnp.concatenate(
                [x[:, s * cols:(s + 1) * cols] for x in by_a[4 * e:4 * e + 4]], axis=1)
    for l2 in range(4):
        by_a = [flat[pl.ds(8 * l2 + a, 8, stride=32), :] for a in range(8)]
        for s in range(2):
            for e in range(2):
                at_row = 16 * l2 + 8 * s
                hs[e, at_row:at_row + 8, :] += jnp.concatenate(
                    [x[:, (2 + s) * cols:(3 + s) * cols] for x in by_a[4 * e:4 * e + 4]], axis=1)
    hole = [lax.dot_general(cm[...], hs[e], (((1,), (0,)), ((), ())), preferred_element_type=F32, precision=highest)
            for e in range(2)]
    for a in range(8):
        hout[pl.ds(a, 64, stride=8), :] = hole[a // 4][:, a % 4 * cols:(a % 4 + 1) * cols]

    spread_group(len(SUMS) - 1)

    for gi in range(len(GROUPS)):
        for way in range(2):
            for part in range(2):
                if hops(way, gi, part) == 4:
                    ring(way, gi, part, 3).wait_send()
    for d in range(OFFSETS):
        swap(d).wait_send()
    wait_bytes(parts.at[pl.ds(0, CHIPS - 1)], r_send)

    def gathered(e):
        low, high = SUMS[e]
        ds = pl.ds(low, high - low)
        wait_bytes(parts.at[:, ds], r_recv.at[e])
        total = parts[0, low:high]
        for n in range(1, CHIPS):
            total = total + parts[n, low:high]
        return [total[n] for n in range(high - low)]

    def col_send(t):
        q = lax.rem(p + t, Z * K)
        return remote(at.at[pl.ds(pl.multiple_of(q * 8, 8), 8), :], slot_a.at[p], f_send, f_recv, q, w)

    def row_send(e, ww):
        src, dst = ((gb, slot_b), (gb4, slot_b4))[e]
        return remote(src.at[ww], dst.at[z], g_send.at[e], g_recv.at[e], m, ww)

    def row_keep(e, ww):
        src, dst = ((gb, slot_b), (gb4, slot_b4))[e]
        return pltpu.make_async_copy(src.at[ww], dst.at[z], g_recv.at[e])

    def rows_start(e):
        for ww in range(W):
            here = jnp.logical_and(m == p, ww == w)
            pl.when(here)(lambda ww=ww: row_keep(e, ww).start())
            pl.when(jnp.logical_not(here))(lambda ww=ww: row_send(e, ww).start())

    def rows_sent(e):
        for ww in range(W):
            here = jnp.logical_and(m == p, ww == w)
            pl.when(jnp.logical_not(here))(lambda ww=ww: row_send(e, ww).wait_send())

    total = sum([gathered(e) for e in range(len(SUMS) - 1)], [])
    for ww in range(W):
        for d in range(1, 4):
            gb[ww, :, (d - 1) * cols:d * cols] = total[d][:, ww * cols:(ww + 1) * cols]
    at[...] = jnp.concatenate(total[:4], axis=0).T
    pltpu.make_async_copy(at.at[pl.ds(pl.multiple_of(p * 8, 8), 8), :], slot_a.at[p], f_recv).start()
    many(1, Z * K, lambda t: col_send(t).start())
    rows_start(0)
    last, = gathered(len(SUMS) - 1)
    for ww in range(W):
        gb4[ww] = last[:, ww * cols:(ww + 1) * cols]
    rows_start(1)

    def result(pair, value):
        out[pair] = value + hout[pair * 8:pair * 8 + 8, :]

    wait_bytes(slot_a, f_recv)
    for zz in range(Z):
        tiles = [slot_a[zz * K + kk] for kk in range(K)]
        for d in range(4):
            result((zz + d) % 8 * 8 + zz, jnp.concatenate([tile[:, d * 8:d * 8 + 8] for tile in tiles], axis=1))
    wait_bytes(slot_b, g_recv.at[0])
    for zz in range(Z):
        tile = slot_b[zz]
        for d in range(1, 4):
            result(zz * 8 + (zz + d) % 8, tile[:, (d - 1) * cols:d * cols])
    wait_bytes(slot_a.at[pl.ds(0, Z * K - 1)], f_send)
    rows_sent(0)
    wait_bytes(slot_b4, g_recv.at[1])
    for zz in range(Z):
        result(zz * 8 + (zz + 4) % 8, slot_b4[zz])
    rows_sent(1)
    wait_bytes(hr.at[pl.ds(0, Z * K - 1)], h_send)


def shards(amplitudes, factors, occ_factors):
    aux_local, rows, virt = factors.shape
    occupied = occ_factors.shape[1]
    local = aux_local // K
    cols = virt // W
    occ = occ_factors.transpose(1, 2, 0).reshape(occupied * occupied, aux_local)
    vm = pl.BlockSpec(memory_space=pltpu.VMEM)
    anywhere = pl.BlockSpec(memory_space=pltpu.HBM)
    dma = pltpu.SemaphoreType.DMA
    v = pltpu.VMEM
    scratch = [
        v((2, virt, virt), F32), v((2, virt, virt), F32),
        v((2 * Z, 8, virt), F32), v((OFFSETS, 8, virt), F32),
        v((OFFSETS, CHIPS, 2, 8, virt), F32), v((local, virt, virt), F32),
        v((OFFSETS, 3 * virt, virt), BF16), v((local, virt, 3 * virt), BF16),
        v((OFFSETS, virt, local * 3 * virt), BF16),
        v((OFFSETS * virt, virt), F32),
        v((OFFSETS, CHIPS, 8, virt), F32), v((OFFSETS, CHIPS, 8, virt), F32),
        v((CHIPS, OFFSETS, 8, virt), F32),
        v((virt, 32), F32),
        v((W, 8, 3 * cols), F32), v((W, 8, cols), F32),
        v((Z * K, 8, 32), F32), v((Z, 8, 3 * cols), F32), v((Z, 8, cols), F32),
        v((virt, 128), F32), v((Z * K, 8, 128), F32),
        v((W, occupied * occupied, aux_local), F32),
        v((64, 64), F32), v((64, 64), F32), v((2, 64, 128), F32), v((64 * 8, cols), F32),
        dma(()), dma((len(GROUPS), K)), dma((len(GROUPS), 2)),
        dma(()), dma(()), dma(()), dma(()), dma(()), dma(()),
        dma((2, len(GROUPS), 2)), dma((2, len(GROUPS), 2, 4)), dma((2, len(GROUPS), 2, 4)),
        dma(()), dma(()), dma(()), dma(()), dma((OFFSETS,)), dma((OFFSETS,)), dma(()), dma((len(SUMS),)), dma(()), dma(()), dma((2,)), dma((2,)),
    ]
    return pl.pallas_call(
        kernel,
        out_shape=jax.ShapeDtypeStruct((occupied * occupied, rows, cols), F32),
        in_specs=[anywhere, anywhere, anywhere],
        out_specs=vm,
        scratch_shapes=scratch,
        compiler_params=pltpu.CompilerParams(
            collective_id=0, has_side_effects=True, vmem_limit_bytes=48 << 20),
        name="residual",
    )(pltpu.with_memory_space_constraint(amplitudes, pltpu.HBM), pltpu.with_memory_space_constraint(factors, pltpu.HBM),
      pltpu.with_memory_space_constraint(occ, pltpu.HBM))


def solution(mesh):
    placed = (P("pairs", None, None), P("aux", "pairs", None), P("aux", None, None))
    return jax.shard_map(
        shards, mesh=mesh, in_specs=placed, out_specs=P(None, "pairs", "aux"), check_vma=False
    )
```
